32 devices in a mesh: clips: 2 (over x), tm: 8 (over z, y), head: 2 (over core).
Axes of the slice: x: 2, y: 2, z: 4, core: 2. Of those that a mesh axis runs over, the one named last changes fastest.
Arguments:
- query: bfloat16 [12288, 3072], P(('clips', 'tm'), 'head'), parts along dimension 0, may hold values from -24 to 24
- key: bfloat16 [12288, 3072], P(('clips', 'tm'), 'head'), parts along dimension 0, may hold values from -12 to 12
- value: bfloat16 [12288, 3072], P(('clips', 'tm'), 'head'), parts along dimension 0, may hold values from -6 to 6
- tile_mask: int32 [16, 6, 27], P(('clips', 'tm')), parts along dimension 0, may hold values from 0 to 1, as said below
- order: int32 [16, 768], P(('clips', 'tm')), parts along dimension 0, may hold values from 0 to 767, each once within a row
- out_weight: bfloat16 [3072, 3072], P(None, 'tm'), may hold values from -0.109375 to 0.109375
Outputs:
- mixed: bfloat16 [12288, 3072], P(('clips', 'tm', 'head')), parts along dimension 0
The draws below stay inside these ranges and needn't reach their ends.
There are 2 independent parts, one for each index of `clips`. The reference program is written for one: setup_inputs(seed, part) draws one part's arguments, and reference() takes and returns one part's arrays. A program takes and returns all parts, laid end to end along the dimension named above; an argument that names none is the same for every part. Nothing has to cross between parts.
Inputs may be any that keep to these rules, and one draw needn't show every extreme that they name: `tile_mask`: the tile itself (slot 13) is always 1; slots of neighbours outside the grid of 8 x 2 x 3 tiles are 0. `order`: each row is a permutation of the 768 rows of one time tile's block.
All inputs are finite; a program needn't handle non-finite values.
Results may differ from the reference program's by a relative error of at most 0.0052.
Values may be sent and summed in bfloat16 or wider, within the bound.
A program may use at most 128 MiB of HBM per device.

```python
import jax
import jax.numpy as jnp
from jax import lax

D = 3072
HEADS = 24
HD = 128
GH = 2
GW = 3
TILE_TOK = 128
SLAB = 768
TT = 8
TOKENS = 6144


def draw_key(key, part):
    inner = jax.random.fold_in(key, 21)
    shape = (TOKENS, HEADS, HD)
    spread = jnp.exp(jax.random.uniform(jax.random.fold_in(inner, 1), (TOKENS, 1, 1), jnp.float32, jnp.log(0.3), jnp.log(3.0)))
    result = jax.random.truncated_normal(jax.random.fold_in(inner, 5), -4.0, 4.0, shape, jnp.float32) * spread
    return result.reshape(TOKENS, HEADS * HD).astype(jnp.bfloat16)


def draw_query(key, part):
    inner = jax.random.fold_in(key, 31)
    shape = (TOKENS, HEADS, HD)
    result = jax.random.truncated_normal(jax.random.fold_in(inner, 4), -6.0, 6.0, shape, jnp.float32)
    return result.reshape(TOKENS, HEADS * HD).astype(jnp.bfloat16)


def draw_tile_mask(key, part):
    count = GH * GW
    times = jnp.arange(TT, dtype=jnp.int32)[:, None, None]
    tiles = jnp.arange(count, dtype=jnp.int32)[None, :, None]
    slots = jnp.arange(27, dtype=jnp.int32)[None, None, :]
    shift_time = slots // 9 - 1
    shift_row = slots // 3 % 3 - 1
    shift_col = slots % 3 - 1
    tile_row = tiles // GW
    tile_col = tiles % GW
    inside = (times + shift_time >= 0) & (times + shift_time < TT)
    inside = inside & (tile_row + shift_row >= 0) & (tile_row + shift_row < GH)
    inside = inside & (tile_col + shift_col >= 0) & (tile_col + shift_col < GW)
    keep = jax.random.randint(jax.random.fold_in(key, 41), (TT, count, 27), 0, 4) > 0
    result = jnp.where(slots == 13, 1, jnp.where(inside & keep, 1, 0))
    return result.astype(jnp.int32)


def level_of(stream_key, extent, pieces, low, largest):
    def one(dim, shards_of):
        draws = jax.random.uniform(jax.random.fold_in(jax.random.fold_in(stream_key, 6), dim), (shards_of,), jnp.float32, low / len(pieces), largest / len(pieces))
        return jnp.repeat(jnp.exp(draws), extent[dim] // shards_of).reshape((-1,) + (1,) * (len(extent) - dim - 1))

    factor_of = one(*pieces[0])
    for cut in pieces[1:]:
        factor_of = factor_of * one(*cut)
    return factor_of


def scatter_about(rng, extent, scale, reach, pieces=(), kind=jnp.bfloat16):
    entries = jax.random.normal(rng, extent, jnp.float32) * scale
    if len(pieces) > 0:
        entries = level_of(rng, extent, pieces, -0.22, 0.18) * entries
    return jnp.clip(entries, min=-reach, max=reach).astype(kind)


def setup_inputs(seed: int = 0, part: int = 0) -> dict:
    splits = jax.random.split(jax.random.key(seed), 7)
    part_splits = jax.random.split(jax.random.fold_in(splits[6], part), 7)
    query = draw_query(jax.random.fold_in(jax.random.fold_in(splits[6], part), 71), part)
    key = draw_key(jax.random.fold_in(jax.random.fold_in(splits[6], part), 71), part)
    value = scatter_about(part_splits[2], (TOKENS, HEADS * HD), 1.0, 6.0, ((0, 8), (1, 2)))
    tile_mask = draw_tile_mask(jax.random.fold_in(jax.random.fold_in(splits[6], part), 71), part)
    order = jax.vmap(lambda own: jax.random.permutation(own, SLAB))(jax.random.split(part_splits[4], TT)).reshape((TT, SLAB)).astype(jnp.int32)
    out_weight = scatter_about(splits[5], (HEADS * HD, D), (HEADS * HD) ** -0.5, 0.109375, ((1, 8),))
    return dict(query=query, key=key, value=value, tile_mask=tile_mask, order=order, out_weight=out_weight)


def allowed_tiles(mask_rows, first_tile, total_tiles):
    count = mask_rows.shape[0]
    tiles = jnp.arange(count, dtype=jnp.int32)
    row_diff = tiles[None, :] // GW - tiles[:, None] // GW
    col_diff = tiles[None, :] % GW - tiles[:, None] % GW
    near = (jnp.abs(row_diff) <= 1) & (jnp.abs(col_diff) <= 1)
    slots = jnp.arange(27, dtype=jnp.int32)
    blocks = []
    for shift_time in (-1, 0, 1):
        slot = (shift_time + 1) * 9 + (jnp.clip(row_diff, -1, 1) + 1) * 3 + jnp.clip(col_diff, -1, 1) + 1
        picked = jnp.sum(jnp.where(slot[:, :, None] == slots[None, None, :], mask_rows[:, None, :], 0), axis=2)
        inside = (first_tile + shift_time >= 0) & (first_tile + shift_time < total_tiles)
        blocks.append(near & (picked == 1) & inside)
    return jnp.stack(blocks, axis=1)


def attend(queries, keys, values, allowed, tile_tok):
    rows = queries.shape[0]
    width = queries.shape[1]
    heads = width // HD
    count = allowed.shape[0]
    head_queries = queries.reshape(rows, heads, HD).transpose(1, 0, 2)
    head_keys = keys.reshape(3 * rows, heads, HD).transpose(1, 0, 2)
    head_values = values.reshape(3 * rows, heads, HD).transpose(1, 0, 2)
    visible = allowed.reshape(count, 1, 3 * count, 1)
    scale = HD ** -0.5

    def one_head(inputs):
        part_q, part_k, part_v = inputs
        scores = jnp.dot(part_q, part_k.T, preferred_element_type=jnp.float32) * scale
        scores = scores.reshape(count, tile_tok, 3 * count, tile_tok)
        scores = jnp.where(visible, scores, -jnp.inf)
        top = jnp.max(scores, axis=(2, 3), keepdims=True)
        expon = jnp.exp(scores - top)
        denom = jnp.sum(expon, axis=(2, 3)).reshape(rows, 1)
        weights = expon.reshape(rows, 3 * rows).astype(jnp.bfloat16)
        result = jnp.dot(weights, part_v, preferred_element_type=jnp.float32) / denom
        return result.astype(jnp.bfloat16)

    outputs = lax.map(one_head, (head_queries, head_keys, head_values))
    return outputs.transpose(1, 0, 2).reshape(rows, width)


def reference(query, key, value, tile_mask, order, out_weight):
    slab = GH * GW * TILE_TOK
    width = HEADS * HD

    def to_tiles(data):
        blocks = data.reshape(TT, slab, width)
        return jnp.take_along_axis(blocks, order[:, :, None], axis=1)

    queries = to_tiles(query)
    keys = to_tiles(key)
    values = to_tiles(value)
    empty = jnp.zeros((1, slab, width), key.dtype)
    keys_pad = jnp.concatenate([empty, keys, empty], axis=0)
    values_pad = jnp.concatenate([empty, values, empty], axis=0)

    def one_tile(index):
        window_keys = lax.dynamic_slice_in_dim(keys_pad, index, 3, 0).reshape(3 * slab, width)
        window_values = lax.dynamic_slice_in_dim(values_pad, index, 3, 0).reshape(3 * slab, width)
        allowed = allowed_tiles(tile_mask[index], index, TT)
        return attend(queries[index], window_keys, window_values, allowed, TILE_TOK)

    tiled = lax.map(one_tile, jnp.arange(TT, dtype=jnp.int32))
    restored = jnp.zeros_like(tiled).at[jnp.arange(TT, dtype=jnp.int32)[:, None], order].set(tiled)
    result = jnp.dot(restored.reshape(TT * slab, width), out_weight, preferred_element_type=jnp.float32)
    return result.astype(jnp.bfloat16)
```

```python
import functools
import math

import jax
import jax.numpy as jnp
from jax import lax
from jax.experimental import pallas as pl
from jax.experimental.pallas import tpu as pltpu
from jax.sharding import PartitionSpec as P

HD = 128
GW = 3
HIDDEN = -1e30
CHUNKS = 3
ROWS = 256
MESH = pl.DeviceIdType.MESH


def when(condition):
    return pl.when(condition)


def kernel(sizes, q_hbm, k_hbm, v_hbm, mask_hbm, order_hbm, w_hbm, out_hbm, *scratch):
    count, heads, slab, tiles, width, cols = sizes
    (kv, qs, hot, qb, ordv, maskv, wt, att, snd, ps, pr, po, ob,
     kv_sem, q_sem, ysend, zsend, ord_recv, ord_send, mask_recv, mask_send,
     w_recv, x_recv, w_up, w_down, w_x, w_y, w_own,
     a_recv, a_send, p_recv, p_send, o_sem) = scratch
    half_heads = heads // 2
    planes = count // 2
    part = width // 2
    piece = part // CHUNKS
    half = slab // 2
    factor = HD ** (-0.5) * math.log2(math.e)

    clip = lax.axis_index("clips")
    me = lax.axis_index("tm")
    core = lax.axis_index("head")
    x = lax.rem(clip, 2)
    z = lax.div(me, 2)
    y = lax.rem(me, 2)
    pair = me + 1 - 2 * y
    sign = 2 * y - 1
    has_up = z < planes - 1
    has_down = z > 0
    has_diag = (z + sign >= 0) & (z + sign < planes)

    to_pair = (clip, pair, core)
    to_up = (clip, me + 2, core)
    to_down = (clip, me - 2, core)
    to_diag = (clip, me + sign, core)
    to_far = (clip, me + 2 * sign, core)
    to_x = (clip + 1 - 2 * x, me, core)
    to_core = (clip, me, 1 - core)

    def remote(src, dst, send, recv, device):
        return pltpu.make_async_remote_copy(
            src_ref=src, dst_ref=dst, send_sem=send, recv_sem=recv,
            device_id=device, device_id_type=MESH,
        )

    def landed(ref, sem):
        pltpu.make_async_copy(ref, ref, sem).wait()

    barrier = pltpu.get_barrier_semaphore()
    for device in (to_pair, to_x, to_core):
        pl.semaphore_signal(barrier, inc=1, device_id=device, device_id_type=MESH)
    for device, valid in ((to_up, has_up), (to_down, has_down), (to_diag, has_diag)):
        @when(valid)
        def _():
            pl.semaphore_signal(barrier, inc=1, device_id=device, device_id_type=MESH)
    pl.semaphore_wait(
        barrier,
        3 + has_up.astype(jnp.int32) + has_down.astype(jnp.int32) + has_diag.astype(jnp.int32),
    )

    def order_copies():
        near = remote(order_hbm, ordv.at[1 + y], ord_send.at[0], ord_recv.at[1 + y], to_pair)
        slot = 3 - 3 * y
        diag = remote(order_hbm, ordv.at[slot], ord_send.at[1], ord_recv.at[slot], to_diag)
        far = remote(order_hbm, ordv.at[slot], ord_send.at[2], ord_recv.at[slot], to_far)
        return near, diag, far

    mask_copy = remote(mask_hbm.at[0], maskv.at[y], mask_send, mask_recv.at[y], to_pair)
    near, diag, far = order_copies()
    near.start()
    mask_copy.start()

    @when(has_diag)
    def _():
        diag.start()
        far.start()

    def pair_copies(head):
        column = pl.ds(pl.multiple_of(((1 - y) * half_heads + head) * HD, HD), HD)
        return [
            remote(k_hbm.at[:, column], kv.at[1 + y, head, 0], ysend.at[head, 0],
                   kv_sem.at[1 + y, head], to_pair),
            remote(v_hbm.at[:, column], kv.at[1 + y, head, 1], ysend.at[head, 1],
                   kv_sem.at[1 + y, head], to_pair),
            remote(q_hbm.at[:, column], qs.at[y, head], ysend.at[head, 2],
                   q_sem.at[y, head], to_pair),
        ]

    def own_rows(step):
        return pl.ds(pl.multiple_of(core * width + x * part + step * piece, piece), piece)

    def wt_rows(side, step):
        return pl.ds(pl.multiple_of(side * part + step * piece, piece), piece)

    def own_weight_copies(step):
        src = w_hbm.at[own_rows(step)]
        dst = wt.at[me, wt_rows(x, step)]
        recv = w_recv.at[me, step]
        return (
            remote(src, dst, w_y.at[step], recv, to_pair),
            remote(src, dst, w_up.at[me, step], recv, to_up),
            remote(src, dst, w_down.at[me, step], recv, to_down),
        )

    own_weight = pltpu.make_async_copy(
        w_hbm.at[pl.ds(pl.multiple_of(core * width, width), width)], wt.at[me], w_own)

    @pl.loop(0, half_heads)
    def _(head):
        for copy in pair_copies(head):
            copy.start()

        @when((head >= 1) & (head <= CHUNKS))
        def _():
            own_weight_copies(head - 1)[0].start()

    @pl.loop(0, CHUNKS)
    def _(step):
        _, up, down = own_weight_copies(step)

        @when(has_up)
        def _():
            up.start()

        @when(has_down)
        def _():
            down.start()

    pltpu.make_async_copy(order_hbm, ordv.at[1 + y], ord_recv.at[1 + y]).start()
    pltpu.make_async_copy(mask_hbm.at[0], maskv.at[y], mask_recv.at[y]).start()

    @pl.loop(0, half_heads)
    def _(head):
        column = pl.ds(pl.multiple_of((y * half_heads + head) * HD, HD), HD)
        pltpu.make_async_copy(k_hbm.at[:, column], kv.at[1 + y, head, 0], kv_sem.at[1 + y, head]).start()
        pltpu.make_async_copy(v_hbm.at[:, column], kv.at[1 + y, head, 1], kv_sem.at[1 + y, head]).start()
        pltpu.make_async_copy(q_hbm.at[:, column], qs.at[y, head], q_sem.at[y, head]).start()

    own_weight.start()

    @when(jnp.logical_not(has_down))
    def _():
        ordv[0] = lax.broadcasted_iota(jnp.int32, (1, slab), 1)

        @pl.loop(0, half_heads)
        def _(head):
            kv[0, head] = jnp.zeros((2, slab, HD), jnp.bfloat16)

    @when(jnp.logical_not(has_up))
    def _():
        ordv[3] = lax.broadcasted_iota(jnp.int32, (1, slab), 1)

        @pl.loop(0, half_heads)
        def _(head):
            kv[3, head] = jnp.zeros((2, slab, HD), jnp.bfloat16)

    @when(has_down)
    def _():
        landed(ordv.at[0], ord_recv.at[0])

    @when(has_up)
    def _():
        landed(ordv.at[3], ord_recv.at[3])

    for slot in (1, 2):
        landed(ordv.at[slot], ord_recv.at[slot])
        landed(maskv.at[slot - 1], mask_recv.at[slot - 1])
    token = lax.broadcasted_iota(jnp.int32, (slab, HD), 0)
    lane = lax.broadcasted_iota(jnp.int32, (slab, HD), 1)
    tile_tok = slab // tiles
    member = jnp.where(lax.div(token, tile_tok) == lane, 1.0, 0.0).astype(jnp.bfloat16)

    @pl.loop(0, 4)
    def _(slot):
        places = ordv[slot]

        @pl.loop(0, slab // HD)
        def _(block):
            row = lax.broadcasted_iota(jnp.int32, (HD, slab), 0) + block * HD
            match = jnp.where(places == row, 1.0, 0.0).astype(jnp.bfloat16)
            hot[slot, pl.ds(pl.multiple_of(block * HD, HD), HD), :] = jnp.dot(
                match, member, preferred_element_type=jnp.float32
            ).astype(jnp.bfloat16)

    tile_row = lax.broadcasted_iota(jnp.int32, (tiles, HD), 0)
    tile_lane = lax.broadcasted_iota(jnp.int32, (tiles, HD), 1)
    row_diff = lax.div(tile_lane, GW) - lax.div(tile_row, GW)
    col_diff = lax.rem(tile_lane, GW) - lax.rem(tile_row, GW)
    near_tiles = (jnp.abs(row_diff) <= 1) & (jnp.abs(col_diff) <= 1) & (tile_lane < tiles)
    place = (row_diff + 1) * 3 + col_diff + 1
    for side in range(2):
        mask = maskv[side]
        for shift in range(3):
            picked = jnp.zeros((tiles, HD), jnp.int32)
            for index in range(9):
                slot = shift * 9 + index
                picked = jnp.where(place == index, mask[:, slot : slot + 1], picked)
            if side == 0 and shift == 0:
                inside = has_down
            elif side == 1 and shift == 2:
                inside = has_up
            else:
                inside = True
            seen = near_tiles & (picked == 1)
            bias = jnp.where(seen, 0.0, HIDDEN)
            if inside is not True:
                bias = jnp.where(inside, bias, HIDDEN)
            bias = jnp.concatenate([bias, jnp.zeros((HD - tiles, HD), jnp.float32)], axis=0)
            qb[side, shift] = jnp.dot(
                hot[1 + side], bias.astype(jnp.bfloat16), preferred_element_type=jnp.float32
            ).astype(jnp.bfloat16)

    def neighbour_copies(head):
        up = remote(kv.at[2, head], kv.at[0, head], zsend.at[0, head], kv_sem.at[0, head], to_up)
        down = remote(kv.at[1, head], kv.at[3, head], zsend.at[1, head], kv_sem.at[3, head], to_down)
        return up, down

    def pass_on(head):
        landed(kv.at[1, head], kv_sem.at[1, head])
        landed(kv.at[2, head], kv_sem.at[2, head])
        up, down = neighbour_copies(head)

        @when(has_up)
        def _():
            up.start()

        @when(has_down)
        def _():
            down.start()

    def weight_copies(tile, step):
        ref = wt.at[tile, wt_rows(x, step)]
        return (
            remote(ref, ref, w_up.at[tile, step], w_recv.at[tile, step], to_up),
            remote(ref, ref, w_down.at[tile, step], w_recv.at[tile, step], to_down),
            remote(ref, ref, w_x.at[tile, step], x_recv.at[tile, step], to_x),
        )

    def relay(event):
        kind, step = lax.div(event, CHUNKS), lax.rem(event, CHUNKS)
        other = lax.rem(kind, 2)
        distance = lax.div(kind, 2) + 1 - other

        @pl.loop(0, 2)
        def _(way):
            plane = z + (2 * way - 1) * distance
            valid = (plane >= 0) & (plane < planes) & ((distance > 0) | (way == 0))

            @when(valid)
            def _():
                tile = 2 * plane + y + other * (1 - 2 * y)
                landed(wt.at[tile, wt_rows(x, step)], w_recv.at[tile, step])
                up, down, across = weight_copies(tile, step)

                @when((plane <= z) & has_up)
                def _():
                    up.start()

                @when((plane >= z) & has_down)
                def _():
                    down.start()

                across.start()

    dims = (((1,), (1,)), ((), ()))
    ones = jnp.ones((slab, HD), jnp.bfloat16)

    def attend(head, side, store):
        @pl.loop(0, slab // ROWS)
        def _(block):
            rows = pl.ds(pl.multiple_of(block * ROWS, ROWS), ROWS)
            queries = qs[side, head, rows, :]
            scores = [
                lax.dot_general(
                    jnp.concatenate([queries, qb[side, shift, rows, :]], axis=1),
                    jnp.concatenate([kv[side + shift, head, 0], hot[side + shift]], axis=1),
                    dims,
                    preferred_element_type=jnp.float32,
                )
                for shift in range(3)
            ]
            top = functools.reduce(
                jnp.maximum, [jnp.max(score, axis=1, keepdims=True) for score in scores]
            )
            total = 0.0
            for shift, score in enumerate(scores):
                expon = jnp.exp2((score - top) * factor).astype(jnp.bfloat16)
                total = total + jnp.dot(
                    expon,
                    jnp.concatenate([kv[side + shift, head, 1], ones], axis=1),
                    preferred_element_type=jnp.float32,
                )
            store(rows, (total[:, :HD] / total[:, HD:]).astype(jnp.bfloat16))

    def result_copy(head):
        column = pl.ds(pl.multiple_of((y * half_heads + head) * HD, HD), HD)
        return remote(snd.at[head], att.at[:, column], a_send.at[head], a_recv.at[head], to_pair)

    pass_on(0)

    @pl.loop(0, half_heads)
    def _(head):
        @when(head + 1 < half_heads)
        def _():
            pass_on(head + 1)

        @when(has_down)
        def _():
            landed(kv.at[0, head], kv_sem.at[0, head])

        @when(has_up)
        def _():
            landed(kv.at[3, head], kv_sem.at[3, head])

        landed(qs.at[0, head], q_sem.at[0, head])
        landed(qs.at[1, head], q_sem.at[1, head])

        def store_other(rows, value):
            snd[head, rows, :] = value

        def store_own(rows, value):
            att[rows, pl.ds(pl.multiple_of((y * half_heads + head) * HD, HD), HD)] = value

        attend(head, 1 - y, store_other)
        result_copy(head).start()
        relay(2 * head)
        attend(head, y, store_own)
        relay(2 * head + 1)

    done = 2 * half_heads

    @pl.loop(0, half_heads)
    def _(head):
        column = pl.ds(pl.multiple_of(((1 - y) * half_heads + head) * HD, HD), HD)
        landed(att.at[:, column], a_recv.at[head])

    landed(wt.at[me], w_own)

    def partial_copy(tile):
        return remote(ps.at[tile], pr.at[tile], p_send.at[tile], p_recv.at[tile], to_core)

    def out_copy(plane):
        column = pl.ds(pl.multiple_of(plane * 2 * cols, 2 * cols), 2 * cols)
        return pltpu.make_async_copy(ob.at[plane], out_hbm.at[:, column], o_sem.at[plane])

    def project(plane):
        @pl.loop(0, 2)
        def _(which):
            tile = 2 * plane + which

            @when(tile != me)
            def _():
                @pl.loop(0, CHUNKS)
                def _(step):
                    landed(wt.at[tile, wt_rows(1 - x, step)], x_recv.at[tile, step])

            rows = pl.ds(pl.multiple_of((1 - core) * half, half), half)
            ps[tile] = jnp.dot(att[rows, :], wt[tile], preferred_element_type=jnp.float32)
            partial_copy(tile).start()

        @pl.loop(0, 2)
        def _(which):
            tile = 2 * plane + which
            rows = pl.ds(pl.multiple_of(core * half, half), half)
            po[tile] = jnp.dot(att[rows, :], wt[tile], preferred_element_type=jnp.float32)

    def finish(plane):
        for which in range(2):
            tile = 2 * plane + which
            landed(pr.at[tile], p_recv.at[tile])
            ob[plane, :, which * cols : (which + 1) * cols] = (po[tile] + pr[tile]).astype(jnp.bfloat16)
        out_copy(plane).start()

    def at_distance(distance, action):
        @pl.loop(0, 2)
        def _(way):
            plane = z + (2 * way - 1) * distance
            valid = (plane >= 0) & (plane < planes) & ((distance > 0) | (way == 0))

            @when(valid)
            def _():
                action(plane)

    events = 2 * planes * CHUNKS

    @pl.loop(0, planes)
    def _(distance):
        @pl.loop(0, 2 * CHUNKS)
        def _(index):
            event = (2 * distance + 2) * CHUNKS + index

            @when((event >= done) & (event < events))
            def _():
                relay(event)

        at_distance(distance, project)

        @when(distance > 0)
        def _():
            at_distance(distance - 1, finish)

    at_distance(planes - 1, finish)

    near.wait_send()
    mask_copy.wait_send()

    @when(has_diag)
    def _():
        diag.wait_send()
        far.wait_send()

    @pl.loop(0, half_heads)
    def _(head):
        for copy in pair_copies(head):
            copy.wait_send()
        up, down = neighbour_copies(head)

        @when(has_up)
        def _():
            up.wait_send()

        @when(has_down)
        def _():
            down.wait_send()

        result_copy(head).wait_send()

    @pl.loop(0, CHUNKS)
    def _(step):
        own_weight_copies(step)[0].wait_send()

        @pl.loop(0, count)
        def _(tile):
            plane = lax.div(tile, 2)
            up, down, across = weight_copies(tile, step)

            @when((plane <= z) & has_up)
            def _():
                up.wait_send()

            @when((plane >= z) & has_down)
            def _():
                down.wait_send()

            @when(tile != me)
            def _():
                across.wait_send()

    @pl.loop(0, count)
    def _(tile):
        partial_copy(tile).wait_send()

    @pl.loop(0, planes)
    def _(plane):
        out_copy(plane).wait()


def on_device(query, key, value, tile_mask, order, out_weight):
    slab, width = query.shape
    tiles = tile_mask.shape[1]
    heads = width // HD
    count = lax.axis_size("tm")
    cols = out_weight.shape[1]
    half_heads = heads // 2
    planes = count // 2
    half = slab // 2
    bf16, f32 = jnp.bfloat16, jnp.float32
    dma = pltpu.SemaphoreType.DMA
    scratch = [
        pltpu.VMEM((4, half_heads, 2, slab, HD), bf16),
        pltpu.VMEM((2, half_heads, slab, HD), bf16),
        pltpu.VMEM((4, slab, HD), bf16),
        pltpu.VMEM((2, 3, slab, HD), bf16),
        pltpu.VMEM((4, 1, slab), jnp.int32),
        pltpu.VMEM((2,) + tile_mask.shape[1:], jnp.int32),
        pltpu.VMEM((count, width, cols), bf16),
        pltpu.VMEM((slab, width), bf16),
        pltpu.VMEM((half_heads, slab, HD), bf16),
        pltpu.VMEM((count, half, cols), f32),
        pltpu.VMEM((count, half, cols), f32),
        pltpu.VMEM((count, half, cols), f32),
        pltpu.VMEM((planes, half, 2 * cols), bf16),
        dma((4, half_heads)),
        dma((2, half_heads)),
        dma((half_heads, 3)),
        dma((2, half_heads)),
        dma((4,)),
        dma((3,)),
        dma((2,)),
        dma,
        dma((count, CHUNKS)),
        dma((count, CHUNKS)),
        dma((count, CHUNKS)),
        dma((count, CHUNKS)),
        dma((count, CHUNKS)),
        dma((CHUNKS,)),
        dma,
        dma((half_heads,)),
        dma((half_heads,)),
        dma((count,)),
        dma((count,)),
        dma((planes,)),
    ]
    sizes = (count, heads, slab, tiles, width, cols)
    return pl.pallas_call(
        functools.partial(kernel, sizes),
        in_specs=[pl.BlockSpec(memory_space=pltpu.HBM)] * 6,
        out_specs=pl.BlockSpec(memory_space=pltpu.HBM),
        out_shape=jax.ShapeDtypeStruct((half, count * cols), bf16),
        scratch_shapes=scratch,
        compiler_params=pltpu.CompilerParams(
            collective_id=0, has_side_effects=True, vmem_limit_bytes=60 << 20
        ),
        cost_estimate=pl.CostEstimate(
            flops=4 * heads * slab * 3 * slab * HD + 2 * slab * width * count * cols,
            bytes_accessed=8 * slab * width,
            transcendentals=heads * slab * 3 * slab,
        ),
        name="clip_attention",
    )(query, key, value, tile_mask, order, out_weight)


def solution(mesh):
    placed = (
        P(("clips", "tm"), "head"),
        P(("clips", "tm"), "head"),
        P(("clips", "tm"), "head"),
        P(("clips", "tm"), None, None),
        P(("clips", "tm"), None),
        P(None, "tm"),
    )
    return jax.shard_map(
        on_device,
        mesh=mesh,
        in_specs=placed,
        out_specs=P(("clips", "tm", "head"), None),
        check_vma=False,
    )
```

```python
import functools
import math

import jax
import jax.numpy as jnp
from jax import lax
from jax.experimental import pallas as pl
from jax.experimental.pallas import tpu as pltpu
from jax.sharding import PartitionSpec as P

HD = 128
GW = 3
HIDDEN = -1e30
CHUNKS = 6
ROWS = 384
OWN_WEIGHT_AFTER = (0, 1, 1, 1, 2, 2)
RELAYS = (5, 5, 0, 1, 7, 1, 4, 4, 6, 0, 1, 3, 0)
MESH = pl.DeviceIdType.MESH


def kernel(sizes, q_hbm, k_hbm, v_hbm, mask_hbm, order_hbm, w_hbm, out_hbm, *scratch):
    count, heads, slab, tiles, width, cols = sizes
    (kv, qs, hot, qb, ordv, maskv, wt, att, snd, qx, qbx, ox, lx, sx, sl, ps, pr, po, ob,
     kv_sem, q_sem, ysend, zsend, ord_recv, ord_send, mask_recv, mask_send,
     w_recv, x_recv, w_up, w_down, w_x, w_y, w_own,
     a_recv, a_send, p_recv, p_send, o_sem,
     qx_recv, qx_send, ox_recv, ox_send, lx_recv, lx_send) = scratch
    half_heads = heads // 2
    planes = count // 2
    part = width // 2
    piece = part // CHUNKS
    half = slab // 2
    factor = HD ** (-0.5) * math.log2(math.e)

    clip = lax.axis_index("clips")
    me = lax.axis_index("tm")
    core = lax.axis_index("head")
    x = lax.rem(clip, 2)
    z = lax.div(me, 2)
    y = lax.rem(me, 2)
    pair = me + 1 - 2 * y
    sign = 2 * y - 1
    has_up = z < planes - 1
    has_down = z > 0
    has_diag = (z + sign >= 0) & (z + sign < planes)
    top, bottom = z == planes - 1, z == 0
    is_end = top | bottom
    helps_top, helps_bottom = z == planes - 2, z == 1
    helps = helps_top | helps_bottom
    merged = jnp.where(top, 0, 1)

    to_pair = (clip, pair, core)
    to_up = (clip, me + 2, core)
    to_down = (clip, me - 2, core)
    to_diag = (clip, me + sign, core)
    to_far = (clip, me + 2 * sign, core)
    to_x = (clip + 1 - 2 * x, me, core)
    to_core = (clip, me, 1 - core)

    def remote(src, dst, send, recv, device):
        return pltpu.make_async_remote_copy(
            src_ref=src, dst_ref=dst, send_sem=send, recv_sem=recv,
            device_id=device, device_id_type=MESH,
        )

    def landed(ref, sem):
        pltpu.make_async_copy(ref, ref, sem).wait()

    barrier = pltpu.get_barrier_semaphore()
    for device in (to_pair, to_x, to_core):
        pl.semaphore_signal(barrier, inc=1, device_id=device, device_id_type=MESH)
    for device, valid in ((to_up, has_up), (to_down, has_down), (to_diag, has_diag)):
        @pl.when(valid)
        def _():
            pl.semaphore_signal(barrier, inc=1, device_id=device, device_id_type=MESH)
    pl.semaphore_wait(
        barrier,
        3 + has_up.astype(jnp.int32) + has_down.astype(jnp.int32) + has_diag.astype(jnp.int32),
    )

    def order_copies():
        near = remote(order_hbm, ordv.at[1 + y], ord_send.at[0], ord_recv.at[1 + y], to_pair)
        slot = 3 - 3 * y
        diag = remote(order_hbm, ordv.at[slot], ord_send.at[1], ord_recv.at[slot], to_diag)
        far = remote(order_hbm, ordv.at[slot], ord_send.at[2], ord_recv.at[slot], to_far)
        return near, diag, far

    mask_copy = remote(mask_hbm.at[0], maskv.at[y], mask_send.at[0], mask_recv.at[y], to_pair)
    mask_diag = remote(mask_hbm.at[0], maskv.at[2], mask_send.at[1], mask_recv.at[2], to_diag)
    mask_far = remote(mask_hbm.at[0], maskv.at[2], mask_send.at[2], mask_recv.at[2], to_far)
    gives_mask = is_end & has_diag
    near, diag, far = order_copies()
    near.start()
    mask_copy.start()

    @pl.when(has_diag)
    def _():
        diag.start()
        far.start()

    @pl.when(gives_mask)
    def _():
        mask_diag.start()
        mask_far.start()

    def pair_copies(head):
        column = pl.ds(pl.multiple_of(((1 - y) * half_heads + head) * HD, HD), HD)
        return [
            remote(k_hbm.at[:, column], kv.at[1 + y, head, 0], ysend.at[head, 0],
                   kv_sem.at[1 + y, head], to_pair),
            remote(v_hbm.at[:, column], kv.at[1 + y, head, 1], ysend.at[head, 1],
                   kv_sem.at[1 + y, head], to_pair),
            remote(q_hbm.at[:, column], qs.at[y, head], ysend.at[head, 2],
                   q_sem.at[y, head], to_pair),
        ]

    def own_rows(step):
        return pl.ds(pl.multiple_of(core * width + x * part + step * piece, piece), piece)

    def wt_rows(side, step):
        return pl.ds(pl.multiple_of(side * part + step * piece, piece), piece)

    def own_weight_copies(step):
        src = w_hbm.at[own_rows(step)]
        dst = wt.at[me, wt_rows(x, step)]
        recv = w_recv.at[me, step]
        return (
            remote(src, dst, w_y.at[step], recv, to_pair),
            remote(src, dst, w_up.at[me, step], recv, to_up),
            remote(src, dst, w_down.at[me, step], recv, to_down),
        )

    own_weight = pltpu.make_async_copy(
        w_hbm.at[pl.ds(pl.multiple_of(core * width, width), width)], wt.at[me], w_own)

    @pl.loop(0, half_heads)
    def _(head):
        for copy in pair_copies(head):
            copy.start()

        for step in range(CHUNKS):
            @pl.when(head == OWN_WEIGHT_AFTER[step])
            def _():
                own_weight_copies(step)[0].start()

    @pl.loop(0, CHUNKS)
    def _(step):
        _, up, down = own_weight_copies(step)

        @pl.when(has_up)
        def _():
            up.start()

        @pl.when(has_down)
        def _():
            down.start()

    pltpu.make_async_copy(order_hbm, ordv.at[1 + y], ord_recv.at[1 + y]).start()
    pltpu.make_async_copy(mask_hbm.at[0], maskv.at[y], mask_recv.at[y]).start()

    @pl.loop(0, half_heads)
    def _(head):
        column = pl.ds(pl.multiple_of((y * half_heads + head) * HD, HD), HD)
        pltpu.make_async_copy(k_hbm.at[:, column], kv.at[1 + y, head, 0], kv_sem.at[1 + y, head]).start()
        pltpu.make_async_copy(v_hbm.at[:, column], kv.at[1 + y, head, 1], kv_sem.at[1 + y, head]).start()
        pltpu.make_async_copy(q_hbm.at[:, column], qs.at[y, head], q_sem.at[y, head]).start()

    own_weight.start()

    @pl.when(bottom)
    def _():
        ordv[0] = lax.broadcasted_iota(jnp.int32, (1, slab), 1)

    @pl.when(top)
    def _():
        ordv[3] = lax.broadcasted_iota(jnp.int32, (1, slab), 1)

    @pl.when(has_down)
    def _():
        landed(ordv.at[0], ord_recv.at[0])

    @pl.when(has_up)
    def _():
        landed(ordv.at[3], ord_recv.at[3])

    for slot in (1, 2):
        landed(ordv.at[slot], ord_recv.at[slot])
        landed(maskv.at[slot - 1], mask_recv.at[slot - 1])
    token = lax.broadcasted_iota(jnp.int32, (slab, HD), 0)
    lane = lax.broadcasted_iota(jnp.int32, (slab, HD), 1)
    tile_tok = slab // tiles
    member = jnp.where(lax.div(token, tile_tok) == lane, 1.0, 0.0).astype(jnp.bfloat16)

    @pl.loop(0, 4)
    def _(slot):
        places = ordv[slot]

        @pl.loop(0, slab // HD)
        def _(block):
            row = lax.broadcasted_iota(jnp.int32, (HD, slab), 0) + block * HD
            match = jnp.where(places == row, 1.0, 0.0).astype(jnp.bfloat16)
            hot[slot, pl.ds(pl.multiple_of(block * HD, HD), HD), :] = jnp.dot(
                match, member, preferred_element_type=jnp.float32
            ).astype(jnp.bfloat16)

    tile_row = lax.broadcasted_iota(jnp.int32, (tiles, HD), 0)
    tile_lane = lax.broadcasted_iota(jnp.int32, (tiles, HD), 1)
    row_diff = lax.div(tile_lane, GW) - lax.div(tile_row, GW)
    col_diff = lax.rem(tile_lane, GW) - lax.rem(tile_row, GW)
    near_tiles = (jnp.abs(row_diff) <= 1) & (jnp.abs(col_diff) <= 1) & (tile_lane < tiles)
    place = (row_diff + 1) * 3 + col_diff + 1

    def bias_of(mask, shift):
        picked = jnp.zeros((tiles, HD), jnp.int32)
        for index in range(9):
            slot = shift * 9 + index
            picked = jnp.where(place == index, mask[:, slot : slot + 1], picked)
        return jnp.where(near_tiles & (picked == 1), 0.0, HIDDEN)

    def bias_rows(slot, bias):
        bias = jnp.concatenate([bias, jnp.zeros((HD - tiles, HD), jnp.float32)], axis=0)
        return jnp.dot(
            hot[slot], bias.astype(jnp.bfloat16), preferred_element_type=jnp.float32
        ).astype(jnp.bfloat16)

    for side in range(2):
        mask = maskv[side]
        for shift in range(3):
            qb[side, shift] = bias_rows(1 + side, bias_of(mask, shift))

    @pl.when(helps)
    def _():
        landed(maskv.at[2], mask_recv.at[2])
        mask = maskv[2]
        bias = jnp.where(helps_top, bias_of(mask, 0), bias_of(mask, 2))
        qbx[...] = bias_rows(jnp.where(helps_top, 3, 0), bias)

    def neighbour_copies(head):
        up = remote(kv.at[2, head], kv.at[0, head], zsend.at[0, head], kv_sem.at[0, head], to_up)
        down = remote(kv.at[1, head], kv.at[3, head], zsend.at[1, head], kv_sem.at[3, head], to_down)
        return up, down

    def query_copies(head):
        def one(device):
            return remote(qs.at[merged, head], qx.at[head], qx_send.at[head], qx_recv.at[head], device)

        return one(to_up), one(to_down)

    def partial_copies(head):
        def one(device):
            return (
                remote(sx.at[head], ox.at[head], ox_send.at[head], ox_recv.at[head], device),
                remote(sl.at[head], lx.at[head], lx_send.at[head], lx_recv.at[head], device),
            )

        return one(to_up), one(to_down)

    def pass_on(head):
        landed(kv.at[1, head], kv_sem.at[1, head])
        landed(kv.at[2, head], kv_sem.at[2, head])
        up, down = neighbour_copies(head)

        @pl.when(has_up & jnp.logical_not(helps_top))
        def _():
            up.start()

        @pl.when(has_down & jnp.logical_not(helps_bottom))
        def _():
            down.start()

        landed(qs.at[0, head], q_sem.at[0, head])
        landed(qs.at[1, head], q_sem.at[1, head])
        up, down = query_copies(head)

        @pl.when(bottom)
        def _():
            up.start()

        @pl.when(top)
        def _():
            down.start()

    def weight_copies(tile, step):
        ref = wt.at[tile, wt_rows(x, step)]
        return (
            remote(ref, ref, w_up.at[tile, step], w_recv.at[tile, step], to_up),
            remote(ref, ref, w_down.at[tile, step], w_recv.at[tile, step], to_down),
            remote(ref, ref, w_x.at[tile, step], x_recv.at[tile, step], to_x),
        )

    def relay(event):
        kind, step = lax.div(event, CHUNKS), lax.rem(event, CHUNKS)
        last = kind == 2 * planes - 2
        other = jnp.where(last, 1, lax.rem(kind, 2))
        distance = jnp.where(last, planes - 1, lax.div(kind, 2) + 1 - other)

        @pl.loop(0, 2)
        def _(way):
            plane = z + (2 * way - 1) * distance
            valid = (plane >= 0) & (plane < planes) & ((distance > 0) | (way == 0))

            @pl.when(valid)
            def _():
                tile = 2 * plane + y + other * (1 - 2 * y)
                landed(wt.at[tile, wt_rows(x, step)], w_recv.at[tile, step])
                up, down, across = weight_copies(tile, step)

                @pl.when((plane <= z) & has_up)
                def _():
                    up.start()

                @pl.when((plane >= z) & has_down)
                def _():
                    down.start()

                across.start()

    dims = (((1,), (1,)), ((), ()))
    ones = jnp.ones((slab, HD), jnp.bfloat16)

    def attend_rows(queries, biases, blocks, head):
        scores = [
            lax.dot_general(
                jnp.concatenate([queries, bias], axis=1),
                jnp.concatenate([kv[block, head, 0], hot[block]], axis=1),
                dims,
                preferred_element_type=jnp.float32,
            )
            for bias, block in zip(biases, blocks)
        ]
        peak = functools.reduce(
            jnp.maximum, [jnp.max(score, axis=1, keepdims=True) for score in scores]
        )
        total = 0.0
        for block, score in zip(blocks, scores):
            expon = jnp.exp2((score - peak) * factor).astype(jnp.bfloat16)
            total = total + jnp.dot(
                expon,
                jnp.concatenate([kv[block, head, 1], ones], axis=1),
                preferred_element_type=jnp.float32,
            )
        denom = total[:, HD:]
        return total[:, :HD] / denom, peak * factor + jnp.log2(denom)

    def over_rows(action):
        @pl.loop(0, slab // ROWS)
        def _(block):
            action(pl.ds(pl.multiple_of(block * ROWS, ROWS), ROWS))

    def store(head, side, rows, value):
        value = value.astype(jnp.bfloat16)

        @pl.when(side == y)
        def _():
            att[rows, pl.ds(pl.multiple_of((y * half_heads + head) * HD, HD), HD)] = value

        @pl.when(side != y)
        def _():
            snd[head, rows, :] = value

    def attend_inner(head, side):
        def action(rows):
            biases = [qb[side, shift, rows, :] for shift in range(3)]
            blocks = [side + shift for shift in range(3)]
            value, _ = attend_rows(qs[side, head, rows, :], biases, blocks, head)
            store(head, side, rows, value)

        over_rows(action)

    def attend_end(head, side, merge):
        def action(rows):
            biases = [qb[side, index + 1 - side, rows, :] for index in range(2)]
            value, level = attend_rows(qs[side, head, rows, :], biases, (1, 2), head)
            if merge:
                other = jnp.broadcast_to(lx[head, 0:1, rows], (HD, ROWS)).T
                high = jnp.maximum(level, other)
                mine, theirs = jnp.exp2(level - high), jnp.exp2(other - high)
                value = (value * mine + ox[head, rows, :].astype(jnp.float32) * theirs) / (mine + theirs)
            store(head, side, rows, value)

        over_rows(action)

    def attend_for_end(head):
        block = jnp.where(helps_top, 2, 1)

        def action(rows):
            value, level = attend_rows(qx[head, rows, :], [qbx[rows, :]], (block,), head)
            sx[head, rows, :] = value.astype(jnp.bfloat16)
            sl[head, :, rows] = level.T[:8, :]

        over_rows(action)

    def result_copy(head):
        column = pl.ds(pl.multiple_of((y * half_heads + head) * HD, HD), HD)
        return remote(snd.at[head], att.at[:, column], a_send.at[head], a_recv.at[head], to_pair)

    def relays_before(point):
        return sum(jnp.where(point > index, many, 0) for index, many in enumerate(RELAYS))

    def relays_at(point):
        @pl.loop(relays_before(point), relays_before(point + 1))
        def _(event):
            relay(event)

    pass_on(0)
    relays_at(0)

    @pl.loop(0, half_heads)
    def _(head):
        @pl.when(head + 1 < half_heads)
        def _():
            pass_on(head + 1)

        @pl.when(helps)
        def _():
            landed(qx.at[head], qx_recv.at[head])
            attend_for_end(head)
            up, down = partial_copies(head)

            @pl.when(helps_top)
            def _():
                for copy in up:
                    copy.start()

            @pl.when(helps_bottom)
            def _():
                for copy in down:
                    copy.start()

        @pl.when(jnp.logical_not(is_end))
        def _():
            landed(kv.at[0, head], kv_sem.at[0, head])
            landed(kv.at[3, head], kv_sem.at[3, head])

        @pl.loop(0, 2)
        def _(turn):
            side = jnp.where(is_end, jnp.where(turn == 0, 1 - merged, merged), jnp.where(turn == 0, 1 - y, y))

            @pl.when(jnp.logical_not(is_end))
            def _():
                attend_inner(head, side)

            @pl.when(is_end & (turn == 0))
            def _():
                attend_end(head, side, False)

            @pl.when(is_end & (turn == 1))
            def _():
                landed(ox.at[head], ox_recv.at[head])
                landed(lx.at[head], lx_recv.at[head])
                attend_end(head, side, True)

            @pl.when(side != y)
            def _():
                result_copy(head).start()

            relays_at(1 + 2 * head + turn)

    done = sum(RELAYS)

    @pl.loop(0, half_heads)
    def _(head):
        column = pl.ds(pl.multiple_of(((1 - y) * half_heads + head) * HD, HD), HD)
        landed(att.at[:, column], a_recv.at[head])

    landed(wt.at[me], w_own)

    def partial_copy(tile):
        return remote(ps.at[tile], pr.at[tile], p_send.at[tile], p_recv.at[tile], to_core)

    def out_copy(plane):
        column = pl.ds(pl.multiple_of(plane * 2 * cols, 2 * cols), 2 * cols)
        return pltpu.make_async_copy(ob.at[plane], out_hbm.at[:, column], o_sem.at[plane])

    def project(plane):
        @pl.loop(0, 2)
        def _(which):
            tile = 2 * plane + which

            @pl.when(tile != me)
            def _():
                @pl.loop(0, CHUNKS)
                def _(step):
                    landed(wt.at[tile, wt_rows(1 - x, step)], x_recv.at[tile, step])

            rows = pl.ds(pl.multiple_of((1 - core) * half, half), half)
            ps[tile] = jnp.dot(att[rows, :], wt[tile], preferred_element_type=jnp.float32)
            partial_copy(tile).start()

        @pl.loop(0, 2)
        def _(which):
            tile = 2 * plane + which
            rows = pl.ds(pl.multiple_of(core * half, half), half)
            po[tile] = jnp.dot(att[rows, :], wt[tile], preferred_element_type=jnp.float32)

    def finish(plane):
        for which in range(2):
            tile = 2 * plane + which
            landed(pr.at[tile], p_recv.at[tile])
            ob[plane, :, which * cols : (which + 1) * cols] = (po[tile] + pr[tile]).astype(jnp.bfloat16)
        out_copy(plane).start()

    def at_distance(distance, action):
        @pl.loop(0, 2)
        def _(way):
            plane = z + (2 * way - 1) * distance
            valid = (plane >= 0) & (plane < planes) & ((distance > 0) | (way == 0))

            @pl.when(valid)
            def _():
                action(plane)

    events = (2 * planes - 1) * CHUNKS

    @pl.loop(0, planes)
    def _(distance):
        @pl.loop(0, 2 * CHUNKS)
        def _(index):
            event = (2 * distance + 2) * CHUNKS + index

            @pl.when((event >= done) & (event < events))
            def _():
                relay(event)

        at_distance(distance, project)

        @pl.when(distance > 0)
        def _():
            at_distance(distance - 1, finish)

    at_distance(planes - 1, finish)

    near.wait_send()
    mask_copy.wait_send()

    @pl.when(gives_mask)
    def _():
        mask_diag.wait_send()
        mask_far.wait_send()

    @pl.when(has_diag)
    def _():
        diag.wait_send()
        far.wait_send()

    @pl.loop(0, half_heads)
    def _(head):
        for copy in pair_copies(head):
            copy.wait_send()
        up, down = neighbour_copies(head)

        @pl.when(has_up & jnp.logical_not(helps_top))
        def _():
            up.wait_send()

        @pl.when(has_down & jnp.logical_not(helps_bottom))
        def _():
            down.wait_send()

        @pl.when(is_end)
        def _():
            query_copies(head)[0].wait_send()

        @pl.when(helps)
        def _():
            for copy in partial_copies(head)[0]:
                copy.wait_send()

        result_copy(head).wait_send()

    @pl.loop(0, CHUNKS)
    def _(step):
        own_weight_copies(step)[0].wait_send()

        @pl.loop(0, count)
        def _(tile):
            plane = lax.div(tile, 2)
            up, down, across = weight_copies(tile, step)

            @pl.when((plane <= z) & has_up)
            def _():
                up.wait_send()

            @pl.when((plane >= z) & has_down)
            def _():
                down.wait_send()

            @pl.when(tile != me)
            def _():
                across.wait_send()

    @pl.loop(0, count)
    def _(tile):
        partial_copy(tile).wait_send()

    @pl.loop(0, planes)
    def _(plane):
        out_copy(plane).wait()


def on_device(query, key, value, tile_mask, order, out_weight):
    slab, width = query.shape
    tiles = tile_mask.shape[1]
    heads = width // HD
    count = lax.axis_size("tm")
    cols = out_weight.shape[1]
    half_heads = heads // 2
    planes = count // 2
    half = slab // 2
    bf16, f32 = jnp.bfloat16, jnp.float32
    dma = pltpu.SemaphoreType.DMA
    scratch = [
        pltpu.VMEM((4, half_heads, 2, slab, HD), bf16),
        pltpu.VMEM((2, half_heads, slab, HD), bf16),
        pltpu.VMEM((4, slab, HD), bf16),
        pltpu.VMEM((2, 3, slab, HD), bf16),
        pltpu.VMEM((4, 1, slab), jnp.int32),
        pltpu.VMEM((3,) + tile_mask.shape[1:], jnp.int32),
        pltpu.VMEM((count, width, cols), bf16),
        pltpu.VMEM((slab, width), bf16),
        pltpu.VMEM((half_heads, slab, HD), bf16),
        pltpu.VMEM((half_heads, slab, HD), bf16),
        pltpu.VMEM((slab, HD), bf16),
        pltpu.VMEM((half_heads, slab, HD), bf16),
        pltpu.VMEM((half_heads, 8, slab), f32),
        pltpu.VMEM((half_heads, slab, HD), bf16),
        pltpu.VMEM((half_heads, 8, slab), f32),
        pltpu.VMEM((count, half, cols), f32),
        pltpu.VMEM((count, half, cols), f32),
        pltpu.VMEM((count, half, cols), f32),
        pltpu.VMEM((planes, half, 2 * cols), bf16),
        dma((4, half_heads)),
        dma((2, half_heads)),
        dma((half_heads, 3)),
        dma((2, half_heads)),
        dma((4,)),
        dma((3,)),
        dma((3,)),
        dma((3,)),
        dma((count, CHUNKS)),
        dma((count, CHUNKS)),
        dma((count, CHUNKS)),
        dma((count, CHUNKS)),
        dma((count, CHUNKS)),
        dma((CHUNKS,)),
        dma,
        dma((half_heads,)),
        dma((half_heads,)),
        dma((count,)),
        dma((count,)),
        dma((planes,)),
        dma((half_heads,)),
        dma((half_heads,)),
        dma((half_heads,)),
        dma((half_heads,)),
        dma((half_heads,)),
        dma((half_heads,)),
    ]
    sizes = (count, heads, slab, tiles, width, cols)
    return pl.pallas_call(
        functools.partial(kernel, sizes),
        in_specs=[pl.BlockSpec(memory_space=pltpu.HBM)] * 6,
        out_specs=pl.BlockSpec(memory_space=pltpu.HBM),
        out_shape=jax.ShapeDtypeStruct((half, count * cols), bf16),
        scratch_shapes=scratch,
        compiler_params=pltpu.CompilerParams(
            collective_id=0, has_side_effects=True, vmem_limit_bytes=60 << 20
        ),
        cost_estimate=pl.CostEstimate(
            flops=4 * heads * slab * 3 * slab * HD + 2 * slab * width * count * cols,
            bytes_accessed=8 * slab * width,
            transcendentals=heads * slab * 3 * slab,
        ),
        name="clip_attention",
    )(query, key, value, tile_mask, order, out_weight)


def solution(mesh):
    placed = (
        P(("clips", "tm"), "head"),
        P(("clips", "tm"), "head"),
        P(("clips", "tm"), "head"),
        P(("clips", "tm"), None, None),
        P(("clips", "tm"), None),
        P(None, "tm"),
    )
    return jax.shard_map(
        on_device,
        mesh=mesh,
        in_specs=placed,
        out_specs=P(("clips", "tm", "head"), None),
        check_vma=False,
    )
```

```python
import functools
import math

import jax
import jax.numpy as jnp
from jax import lax
from jax.experimental import pallas as pl
from jax.experimental.pallas import tpu as pltpu
from jax.sharding import PartitionSpec as P

HD = 128
GW = 3
HIDDEN = -1e30
CHUNKS = 6
ROWS = 384
OWN_WEIGHT_AFTER = (0, 0, 1, 1, 2, 2)
RELAYS = (6, 3, 1, 3, 4, 2, 4, 9, 3, 1, 1, 0, 5)
MESH = pl.DeviceIdType.MESH


def kernel(sizes, q_hbm, k_hbm, v_hbm, mask_hbm, order_hbm, w_hbm, out_hbm, *scratch):
    count, heads, slab, tiles, width, cols = sizes
    (kv, qs, hot, qb, ordv, maskv, wt, att, snd, qx, qbx, ox, lx, sx, sl, ps, pr, po, ob,
     kv_sem, q_sem, ysend, zsend, ord_recv, ord_send, mask_recv, mask_send,
     w_recv, x_recv, w_up, w_down, w_x, w_y, w_own,
     a_recv, a_send, p_recv, p_send, o_sem,
     qx_recv, qx_send, ox_recv, ox_send, lx_recv, lx_send) = scratch
    half_heads = heads // 2
    planes = count // 2
    part = width // 2
    piece = part // CHUNKS
    half = slab // 2
    factor = HD ** (-0.5) * math.log2(math.e)

    clip = lax.axis_index("clips")
    me = lax.axis_index("tm")
    core = lax.axis_index("head")
    x = lax.rem(clip, 2)
    z = lax.div(me, 2)
    y = lax.rem(me, 2)
    pair = me + 1 - 2 * y
    sign = 2 * y - 1
    has_up = z < planes - 1
    has_down = z > 0
    has_diag = (z + sign >= 0) & (z + sign < planes)
    top, bottom = z == planes - 1, z == 0
    is_end = top | bottom
    helps_top, helps_bottom = z == planes - 2, z == 1
    helps = helps_top | helps_bottom
    merged = jnp.where(top, 0, 1)

    to_pair = (clip, pair, core)
    to_up = (clip, me + 2, core)
    to_down = (clip, me - 2, core)
    to_diag = (clip, me + sign, core)
    to_far = (clip, me + 2 * sign, core)
    to_x = (clip + 1 - 2 * x, me, core)
    to_core = (clip, me, 1 - core)

    def remote(src, dst, send, recv, device):
        return pltpu.make_async_remote_copy(
            src_ref=src, dst_ref=dst, send_sem=send, recv_sem=recv,
            device_id=device, device_id_type=MESH,
        )

    def landed(ref, sem):
        pltpu.make_async_copy(ref, ref, sem).wait()

    barrier = pltpu.get_barrier_semaphore()
    for device in (to_pair, to_x, to_core):
        pl.semaphore_signal(barrier, inc=1, device_id=device, device_id_type=MESH)
    for device, valid in ((to_up, has_up), (to_down, has_down), (to_diag, has_diag)):
        @pl.when(valid)
        def _():
            pl.semaphore_signal(barrier, inc=1, device_id=device, device_id_type=MESH)
    pl.semaphore_wait(
        barrier,
        3 + has_up.astype(jnp.int32) + has_down.astype(jnp.int32) + has_diag.astype(jnp.int32),
    )

    def order_copies():
        near = remote(order_hbm, ordv.at[1 + y], ord_send.at[0], ord_recv.at[1 + y], to_pair)
        slot = 3 - 3 * y
        diag = remote(order_hbm, ordv.at[slot], ord_send.at[1], ord_recv.at[slot], to_diag)
        far = remote(order_hbm, ordv.at[slot], ord_send.at[2], ord_recv.at[slot], to_far)
        return near, diag, far

    mask_copy = remote(mask_hbm, maskv.at[y], mask_send.at[0], mask_recv.at[y], to_pair)
    mask_diag = remote(mask_hbm, maskv.at[2], mask_send.at[1], mask_recv.at[2], to_diag)
    mask_far = remote(mask_hbm, maskv.at[2], mask_send.at[2], mask_recv.at[2], to_far)
    gives_mask = is_end & has_diag
    near, diag, far = order_copies()
    near.start()
    mask_copy.start()

    @pl.when(has_diag)
    def _():
        diag.start()
        far.start()

    @pl.when(gives_mask)
    def _():
        mask_diag.start()
        mask_far.start()

    def pair_copies(head):
        column = pl.ds(pl.multiple_of(((1 - y) * half_heads + head) * HD, HD), HD)
        return [
            remote(k_hbm.at[:, column], kv.at[1 + y, head, 0], ysend.at[head, 0],
                   kv_sem.at[1 + y, head], to_pair),
            remote(v_hbm.at[:, column], kv.at[1 + y, head, 1], ysend.at[head, 1],
                   kv_sem.at[1 + y, head], to_pair),
            remote(q_hbm.at[:, column], qs.at[y, head], ysend.at[head, 2],
                   q_sem.at[y, head], to_pair),
        ]

    def own_rows(step):
        return pl.ds(pl.multiple_of(core * width + x * part + step * piece, piece), piece)

    def wt_rows(side, step):
        return pl.ds(pl.multiple_of(side * part + step * piece, piece), piece)

    def wt_part(tile, side):
        return wt.at[tile, pl.ds(pl.multiple_of(side * part, part), part)]

    def own_weight_copies(step):
        src = w_hbm.at[own_rows(step)]
        dst = wt.at[me, wt_rows(x, step)]
        recv = w_recv.at[me, step]
        return (
            remote(src, dst, w_y, recv, to_pair),
            remote(src, dst, w_up.at[me], recv, to_up),
            remote(src, dst, w_down.at[me], recv, to_down),
        )

    own_weight = pltpu.make_async_copy(
        w_hbm.at[pl.ds(pl.multiple_of(core * width, width), width)], wt.at[me], w_own)

    @pl.loop(0, half_heads)
    def _(head):
        for copy in pair_copies(head):
            copy.start()

        for step in range(CHUNKS):
            @pl.when(head == OWN_WEIGHT_AFTER[step])
            def _():
                own_weight_copies(step)[0].start()

    @pl.loop(0, CHUNKS)
    def _(step):
        _, up, down = own_weight_copies(step)

        @pl.when(has_up)
        def _():
            up.start()

        @pl.when(has_down)
        def _():
            down.start()

    pltpu.make_async_copy(order_hbm, ordv.at[1 + y], ord_recv.at[1 + y]).start()
    pltpu.make_async_copy(mask_hbm, maskv.at[y], mask_recv.at[y]).start()

    @pl.loop(0, half_heads)
    def _(head):
        column = pl.ds(pl.multiple_of((y * half_heads + head) * HD, HD), HD)
        pltpu.make_async_copy(k_hbm.at[:, column], kv.at[1 + y, head, 0], kv_sem.at[1 + y, head]).start()
        pltpu.make_async_copy(v_hbm.at[:, column], kv.at[1 + y, head, 1], kv_sem.at[1 + y, head]).start()
        pltpu.make_async_copy(q_hbm.at[:, column], qs.at[y, head], q_sem.at[y, head]).start()

    own_weight.start()

    @pl.when(bottom)
    def _():
        ordv[0] = lax.broadcasted_iota(jnp.int32, (1, slab), 1)

    @pl.when(top)
    def _():
        ordv[3] = lax.broadcasted_iota(jnp.int32, (1, slab), 1)

    @pl.when(has_down)
    def _():
        landed(ordv.at[0], ord_recv.at[0])

    @pl.when(has_up)
    def _():
        landed(ordv.at[3], ord_recv.at[3])

    for slot in (1, 2):
        landed(ordv.at[slot], ord_recv.at[slot])
        landed(maskv.at[slot - 1], mask_recv.at[slot - 1])
    token = lax.broadcasted_iota(jnp.int32, (slab, HD), 0)
    lane = lax.broadcasted_iota(jnp.int32, (slab, HD), 1)
    tile_tok = slab // tiles
    member = jnp.where(lax.div(token, tile_tok) == lane, 1.0, 0.0).astype(jnp.bfloat16)

    @pl.loop(0, 4)
    def _(slot):
        places = ordv[slot]

        @pl.loop(0, slab // HD)
        def _(block):
            row = lax.broadcasted_iota(jnp.int32, (HD, slab), 0) + block * HD
            match = jnp.where(places == row, 1.0, 0.0).astype(jnp.bfloat16)
            hot[slot, pl.ds(pl.multiple_of(block * HD, HD), HD), :] = jnp.dot(
                match, member, preferred_element_type=jnp.float32
            ).astype(jnp.bfloat16)

    tile_row = lax.broadcasted_iota(jnp.int32, (tiles, HD), 0)
    tile_lane = lax.broadcasted_iota(jnp.int32, (tiles, HD), 1)
    row_diff = lax.div(tile_lane, GW) - lax.div(tile_row, GW)
    col_diff = lax.rem(tile_lane, GW) - lax.rem(tile_row, GW)
    near_tiles = (jnp.abs(row_diff) <= 1) & (jnp.abs(col_diff) <= 1) & (tile_lane < tiles)
    place = (row_diff + 1) * 3 + col_diff + 1

    def mask_rows(slot):
        return jnp.concatenate([maskv[slot, tile] for tile in range(tiles)], axis=0)

    def bias_of(mask, shift):
        picked = jnp.zeros((tiles, HD), jnp.int32)
        for index in range(9):
            slot = shift * 9 + index
            picked = jnp.where(place == index, mask[:, slot : slot + 1], picked)
        return jnp.where(near_tiles & (picked == 1), 0.0, HIDDEN)

    def bias_rows(slot, bias):
        bias = jnp.concatenate([bias, jnp.zeros((HD - tiles, HD), jnp.float32)], axis=0)
        return jnp.dot(
            hot[slot], bias.astype(jnp.bfloat16), preferred_element_type=jnp.float32
        ).astype(jnp.bfloat16)

    for side in range(2):
        mask = mask_rows(side)
        for shift in range(3):
            qb[side, shift] = bias_rows(1 + side, bias_of(mask, shift))

    @pl.when(helps)
    def _():
        landed(maskv.at[2], mask_recv.at[2])
        mask = mask_rows(2)
        bias = jnp.where(helps_top, bias_of(mask, 0), bias_of(mask, 2))
        qbx[...] = bias_rows(jnp.where(helps_top, 3, 0), bias)

    def neighbour_copies(head):
        up = remote(kv.at[2, head], kv.at[0, head], zsend.at[0, head], kv_sem.at[0, head], to_up)
        down = remote(kv.at[1, head], kv.at[3, head], zsend.at[1, head], kv_sem.at[3, head], to_down)
        return up, down

    def query_copies(head):
        def one(device):
            return remote(qs.at[merged, head], qx.at[head], qx_send.at[head], qx_recv.at[head], device)

        return one(to_up), one(to_down)

    def partial_copies(head):
        def one(device):
            return (
                remote(sx.at[head], ox.at[head], ox_send.at[head], ox_recv.at[head], device),
                remote(sl.at[head], lx.at[head], lx_send.at[head], lx_recv.at[head], device),
            )

        return one(to_up), one(to_down)

    def pass_on(head):
        landed(kv.at[1, head], kv_sem.at[1, head])
        landed(kv.at[2, head], kv_sem.at[2, head])
        up, down = neighbour_copies(head)

        @pl.when(has_up & jnp.logical_not(helps_top))
        def _():
            up.start()

        @pl.when(has_down & jnp.logical_not(helps_bottom))
        def _():
            down.start()

        landed(qs.at[0, head], q_sem.at[0, head])
        landed(qs.at[1, head], q_sem.at[1, head])
        up, down = query_copies(head)

        @pl.when(bottom)
        def _():
            up.start()

        @pl.when(top)
        def _():
            down.start()

    def weight_copies(tile, step):
        ref = wt.at[tile, wt_rows(x, step)]
        return (
            remote(ref, ref, w_up.at[tile], w_recv.at[tile, step], to_up),
            remote(ref, ref, w_down.at[tile], w_recv.at[tile, step], to_down),
            remote(ref, ref, w_x.at[tile], x_recv.at[tile], to_x),
        )

    def relay(event):
        kind, step = lax.div(event, CHUNKS), lax.rem(event, CHUNKS)
        last = kind == 2 * planes - 2
        other = jnp.where(last, 1, lax.rem(kind, 2))
        distance = jnp.where(last, planes - 1, lax.div(kind, 2) + 1 - other)

        @pl.loop(0, 2)
        def _(way):
            plane = z + (2 * way - 1) * distance
            valid = (plane >= 0) & (plane < planes) & ((distance > 0) | (way == 0))

            @pl.when(valid)
            def _():
                tile = 2 * plane + y + other * (1 - 2 * y)
                landed(wt.at[tile, wt_rows(x, step)], w_recv.at[tile, step])
                up, down, across = weight_copies(tile, step)

                @pl.when((plane <= z) & has_up)
                def _():
                    up.start()

                @pl.when((plane >= z) & has_down)
                def _():
                    down.start()

                across.start()

    dims = (((1,), (1,)), ((), ()))
    ones = jnp.ones((slab, HD), jnp.bfloat16)

    def attend_rows(queries, biases, blocks, head):
        peak = total = None
        for bias, block in zip(biases, blocks):
            score = lax.dot_general(
                jnp.concatenate([queries, bias], axis=1),
                jnp.concatenate([kv[block, head, 0], hot[block]], axis=1),
                dims,
                preferred_element_type=jnp.float32,
            )
            before, peak = peak, jnp.max(score, axis=1, keepdims=True)
            if before is not None:
                peak = jnp.maximum(before, peak)
            part_sum = jnp.dot(
                jnp.exp2((score - peak) * factor).astype(jnp.bfloat16),
                jnp.concatenate([kv[block, head, 1], ones], axis=1),
                preferred_element_type=jnp.float32,
            )
            total = part_sum if before is None else total * jnp.exp2((before - peak) * factor) + part_sum
        denom = total[:, HD:]
        return total[:, :HD] / denom, peak * factor + jnp.log2(denom)

    def over_rows(action):
        @pl.loop(0, slab // ROWS)
        def _(block):
            action(pl.ds(pl.multiple_of(block * ROWS, ROWS), ROWS))

    def store(head, side, rows, value):
        value = value.astype(jnp.bfloat16)

        @pl.when(side == y)
        def _():
            att[rows, pl.ds(pl.multiple_of((y * half_heads + head) * HD, HD), HD)] = value

        @pl.when(side != y)
        def _():
            snd[head, rows, :] = value

    def attend_inner(head, side):
        def action(rows):
            biases = [qb[side, shift, rows, :] for shift in range(3)]
            blocks = [side + shift for shift in range(3)]
            value, _ = attend_rows(qs[side, head, rows, :], biases, blocks, head)
            store(head, side, rows, value)

        over_rows(action)

    def attend_end(head, side, merge):
        def action(rows):
            biases = [qb[side, index + 1 - side, rows, :] for index in range(2)]
            value, level = attend_rows(qs[side, head, rows, :], biases, (1, 2), head)
            if merge:
                other = jnp.broadcast_to(lx[head, 0:1, rows], (HD, ROWS)).T
                high = jnp.maximum(level, other)
                mine, theirs = jnp.exp2(level - high), jnp.exp2(other - high)
                value = (value * mine + ox[head, rows, :].astype(jnp.float32) * theirs) / (mine + theirs)
            store(head, side, rows, value)

        over_rows(action)

    def attend_for_end(head):
        block = jnp.where(helps_top, 2, 1)

        def action(rows):
            value, level = attend_rows(qx[head, rows, :], [qbx[rows, :]], (block,), head)
            sx[head, rows, :] = value.astype(jnp.bfloat16)
            sl[head, :, rows] = level.T[:8, :]

        over_rows(action)

    def result_copy(head):
        column = pl.ds(pl.multiple_of((y * half_heads + head) * HD, HD), HD)
        return remote(snd.at[head], att.at[:, column], a_send.at[head], a_recv.at[head], to_pair)

    def relays_before(point):
        return sum(jnp.where(point > index, many, 0) for index, many in enumerate(RELAYS))

    def relays_at(point):
        @pl.loop(relays_before(point), relays_before(point + 1))
        def _(event):
            relay(event)

    pass_on(0)
    relays_at(0)

    @pl.loop(0, half_heads)
    def _(head):
        @pl.when(head + 1 < half_heads)
        def _():
            pass_on(head + 1)

        @pl.when(helps)
        def _():
            landed(qx.at[head], qx_recv.at[head])
            attend_for_end(head)
            up, down = partial_copies(head)

            @pl.when(helps_top)
            def _():
                for copy in up:
                    copy.start()

            @pl.when(helps_bottom)
            def _():
                for copy in down:
                    copy.start()

        @pl.when(jnp.logical_not(is_end))
        def _():
            landed(kv.at[0, head], kv_sem.at[0, head])
            landed(kv.at[3, head], kv_sem.at[3, head])

        @pl.loop(0, 2)
        def _(turn):
            side = jnp.where(is_end, jnp.where(turn == 0, 1 - merged, merged), jnp.where(turn == 0, 1 - y, y))

            @pl.when(jnp.logical_not(is_end))
            def _():
                attend_inner(head, side)

            @pl.when(is_end & (turn == 0))
            def _():
                attend_end(head, side, False)

            @pl.when(is_end & (turn == 1))
            def _():
                landed(ox.at[head], ox_recv.at[head])
                landed(lx.at[head], lx_recv.at[head])
                attend_end(head, side, True)

            @pl.when(side != y)
            def _():
                result_copy(head).start()

            relays_at(1 + 2 * head + turn)

    done = sum(RELAYS)

    near.wait_send()
    mask_copy.wait_send()

    @pl.when(gives_mask)
    def _():
        mask_diag.wait_send()
        mask_far.wait_send()

    @pl.when(has_diag)
    def _():
        diag.wait_send()
        far.wait_send()

    @pl.loop(0, half_heads)
    def _(head):
        for copy in pair_copies(head):
            copy.wait_send()
        up, down = neighbour_copies(head)

        @pl.when(has_up & jnp.logical_not(helps_top))
        def _():
            up.wait_send()

        @pl.when(has_down & jnp.logical_not(helps_bottom))
        def _():
            down.wait_send()

        @pl.when(is_end)
        def _():
            query_copies(head)[0].wait_send()

        @pl.when(helps)
        def _():
            for copy in partial_copies(head)[0]:
                copy.wait_send()

    def left(ref, sem):
        remote(ref, ref, sem, x_recv.at[me], to_x).wait_send()

    left(wt_part(me, x), w_y)

    def sent_results():
        @pl.loop(0, half_heads)
        def _(head):
            result_copy(head).wait_send()

    def sent_weights():
        @pl.loop(0, count)
        def _(tile):
            plane = lax.div(tile, 2)

            @pl.when((plane <= z) & has_up)
            def _():
                left(wt_part(tile, x), w_up.at[tile])

            @pl.when((plane >= z) & has_down)
            def _():
                left(wt_part(tile, x), w_down.at[tile])

            @pl.when(tile != me)
            def _():
                left(wt_part(tile, x), w_x.at[tile])


    @pl.loop(0, half_heads)
    def _(head):
        column = pl.ds(pl.multiple_of(((1 - y) * half_heads + head) * HD, HD), HD)
        landed(att.at[:, column], a_recv.at[head])

    landed(wt.at[me], w_own)

    def partial_copy(tile):
        return remote(ps.at[tile], pr.at[tile], p_send.at[tile], p_recv.at[tile], to_core)

    def out_copy(plane):
        column = pl.ds(pl.multiple_of(plane * 2 * cols, 2 * cols), 2 * cols)
        return pltpu.make_async_copy(ob.at[plane], out_hbm.at[:, column], o_sem.at[plane])

    def project(plane):
        @pl.loop(0, 2)
        def _(which):
            tile = 2 * plane + which

            @pl.when(tile != me)
            def _():
                landed(wt_part(tile, 1 - x), x_recv.at[tile])

            rows = pl.ds(pl.multiple_of((1 - core) * half, half), half)
            ps[tile] = jnp.dot(att[rows, :], wt[tile], preferred_element_type=jnp.float32)
            partial_copy(tile).start()

        @pl.loop(0, 2)
        def _(which):
            tile = 2 * plane + which
            rows = pl.ds(pl.multiple_of(core * half, half), half)
            po[tile] = jnp.dot(att[rows, :], wt[tile], preferred_element_type=jnp.float32)

    def finish(plane):
        for which in range(2):
            tile = 2 * plane + which
            landed(pr.at[tile], p_recv.at[tile])
            ob[plane, :, which * cols : (which + 1) * cols] = (po[tile] + pr[tile]).astype(jnp.bfloat16)
        out_copy(plane).start()

    def at_distance(distance, action):
        @pl.loop(0, 2)
        def _(way):
            plane = z + (2 * way - 1) * distance
            valid = (plane >= 0) & (plane < planes) & ((distance > 0) | (way == 0))

            @pl.when(valid)
            def _():
                action(plane)

    events = (2 * planes - 1) * CHUNKS

    @pl.loop(0, planes)
    def _(distance):
        @pl.loop(0, 2 * CHUNKS)
        def _(index):
            event = (2 * distance + 2) * CHUNKS + index

            @pl.when((event >= done) & (event < events))
            def _():
                relay(event)

        at_distance(distance, project)

        @pl.when(distance > 0)
        def _():
            at_distance(distance - 1, finish)

    at_distance(planes - 1, finish)

    sent_results()
    sent_weights()

    @pl.loop(0, count)
    def _(tile):
        partial_copy(tile).wait_send()

    @pl.loop(0, planes)
    def _(plane):
        out_copy(plane).wait()


def on_device(query, key, value, tile_mask, order, out_weight):
    slab, width = query.shape
    tiles = tile_mask.shape[1]
    heads = width // HD
    count = lax.axis_size("tm")
    cols = out_weight.shape[1]
    half_heads = heads // 2
    planes = count // 2
    half = slab // 2
    bf16, f32 = jnp.bfloat16, jnp.float32
    dma = pltpu.SemaphoreType.DMA
    scratch = [
        pltpu.VMEM((4, half_heads, 2, slab, HD), bf16),
        pltpu.VMEM((2, half_heads, slab, HD), bf16),
        pltpu.VMEM((4, slab, HD), bf16),
        pltpu.VMEM((2, 3, slab, HD), bf16),
        pltpu.VMEM((4, 1, slab), jnp.int32),
        pltpu.VMEM((3, tiles, 1, tile_mask.shape[2]), jnp.int32),
        pltpu.VMEM((count, width, cols), bf16),
        pltpu.VMEM((slab, width), bf16),
        pltpu.VMEM((half_heads, slab, HD), bf16),
        pltpu.VMEM((half_heads, slab, HD), bf16),
        pltpu.VMEM((slab, HD), bf16),
        pltpu.VMEM((half_heads, slab, HD), bf16),
        pltpu.VMEM((half_heads, 8, slab), f32),
        pltpu.VMEM((half_heads, slab, HD), bf16),
        pltpu.VMEM((half_heads, 8, slab), f32),
        pltpu.VMEM((count, half, cols), f32),
        pltpu.VMEM((count, half, cols), f32),
        pltpu.VMEM((count, half, cols), f32),
        pltpu.VMEM((planes, half, 2 * cols), bf16),
        dma((4, half_heads)),
        dma((2, half_heads)),
        dma((half_heads, 3)),
        dma((2, half_heads)),
        dma((4,)),
        dma((3,)),
        dma((3,)),
        dma((3,)),
        dma((count, CHUNKS)),
        dma((count,)),
        dma((count,)),
        dma((count,)),
        dma((count,)),
        dma,
        dma,
        dma((half_heads,)),
        dma((half_heads,)),
        dma((count,)),
        dma((count,)),
        dma((planes,)),
        dma((half_heads,)),
        dma((half_heads,)),
        dma((half_heads,)),
        dma((half_heads,)),
        dma((half_heads,)),
        dma((half_heads,)),
    ]
    sizes = (count, heads, slab, tiles, width, cols)
    return pl.pallas_call(
        functools.partial(kernel, sizes),
        in_specs=[pl.BlockSpec(memory_space=pltpu.HBM)] * 6,
        out_specs=pl.BlockSpec(memory_space=pltpu.HBM),
        out_shape=jax.ShapeDtypeStruct((half, count * cols), bf16),
        scratch_shapes=scratch,
        compiler_params=pltpu.CompilerParams(
            collective_id=0, has_side_effects=True, vmem_limit_bytes=60 << 20
        ),
        cost_estimate=pl.CostEstimate(
            flops=4 * heads * slab * 3 * slab * HD + 2 * slab * width * count * cols,
            bytes_accessed=8 * slab * width,
            transcendentals=heads * slab * 3 * slab,
        ),
        name="clip_attention",
    )(query, key, value, tile_mask.transpose(1, 0, 2), order, out_weight)


def solution(mesh):
    placed = (
        P(("clips", "tm"), "head"),
        P(("clips", "tm"), "head"),
        P(("clips", "tm"), "head"),
        P(("clips", "tm"), None, None),
        P(("clips", "tm"), None),
        P(None, "tm"),
    )
    return jax.shard_map(
        on_device,
        mesh=mesh,
        in_specs=placed,
        out_specs=P(("clips", "tm", "head"), None),
        check_vma=False,
    )
```

```python
import functools
import math

import jax
import jax.numpy as jnp
from jax import lax
from jax.experimental import pallas as pl
from jax.experimental.pallas import tpu as pltpu
from jax.sharding import PartitionSpec as P

HD = 128
GW = 3
HIDDEN = -1e30
CHUNKS = 3
ROWS = 768
LATE = 2
EARLY_DISTANCE = 2
OWN_WEIGHT_AFTER = (0, 0, 1)
RELAYS = (5, 3, 0, 0, 2, 5, 0, 2, 0, 4, 0, 0, 0)
MESH = pl.DeviceIdType.MESH


def kernel(sizes, q_hbm, k_hbm, v_hbm, mask_hbm, order_hbm, w_hbm, out_hbm, *scratch):
    count, heads, slab, tiles, width, cols = sizes
    (kv, qs, hot, qb, ordv, maskv, wt, att, snd, qx, qbx, ox, lx, sx, sl, ps, pr, po, ob,
     kv_sem, q_sem, ysend, zsend, ord_recv, ord_send, mask_recv, mask_send,
     w_recv, x_recv, w_up, w_down, w_x, w_y, w_own,
     a_recv, a_send, p_recv, p_send, o_sem,
     qx_recv, qx_send, ox_recv, ox_send, lx_recv, lx_send) = scratch
    half_heads = heads // 2
    planes = count // 2
    part = width // 2
    piece = part // CHUNKS
    half = slab // 2
    factor = HD ** (-0.5) * math.log2(math.e)

    clip = lax.axis_index("clips")
    me = lax.axis_index("tm")
    core = lax.axis_index("head")
    x = lax.rem(clip, 2)
    z = lax.div(me, 2)
    y = lax.rem(me, 2)
    pair = me + 1 - 2 * y
    sign = 2 * y - 1
    has_up = z < planes - 1
    has_down = z > 0
    has_diag = (z + sign >= 0) & (z + sign < planes)
    top, bottom = z == planes - 1, z == 0
    is_end = top | bottom
    helps_top, helps_bottom = z == planes - 2, z == 1
    helps = helps_top | helps_bottom
    merged = jnp.where(top, 0, 1)

    to_pair = (clip, pair, core)
    to_up = (clip, me + 2, core)
    to_down = (clip, me - 2, core)
    to_diag = (clip, me + sign, core)
    to_far = (clip, me + 2 * sign, core)
    to_x = (clip + 1 - 2 * x, me, core)
    to_core = (clip, me, 1 - core)

    def remote(src, dst, send, recv, device):
        return pltpu.make_async_remote_copy(
            src_ref=src, dst_ref=dst, send_sem=send, recv_sem=recv,
            device_id=device, device_id_type=MESH,
        )

    def landed(ref, sem):
        pltpu.make_async_copy(ref, ref, sem).wait()

    barrier = pltpu.get_barrier_semaphore()
    for device in (to_pair, to_x, to_core):
        pl.semaphore_signal(barrier, inc=1, device_id=device, device_id_type=MESH)
    for device, valid in ((to_up, has_up), (to_down, has_down), (to_diag, has_diag)):
        @pl.when(valid)
        def _():
            pl.semaphore_signal(barrier, inc=1, device_id=device, device_id_type=MESH)
    pl.semaphore_wait(
        barrier,
        3 + has_up.astype(jnp.int32) + has_down.astype(jnp.int32) + has_diag.astype(jnp.int32),
    )

    def order_copies():
        near = remote(order_hbm, ordv.at[1 + y], ord_send.at[0], ord_recv.at[1 + y], to_pair)
        slot = 3 - 3 * y
        diag = remote(order_hbm, ordv.at[slot], ord_send.at[1], ord_recv.at[slot], to_diag)
        far = remote(order_hbm, ordv.at[slot], ord_send.at[2], ord_recv.at[slot], to_far)
        return near, diag, far

    mask_copy = remote(mask_hbm, maskv.at[y], mask_send.at[0], mask_recv.at[y], to_pair)
    mask_diag = remote(mask_hbm, maskv.at[2], mask_send.at[1], mask_recv.at[2], to_diag)
    mask_far = remote(mask_hbm, maskv.at[2], mask_send.at[2], mask_recv.at[2], to_far)
    gives_mask = is_end & has_diag
    near, diag, far = order_copies()
    near.start()
    mask_copy.start()

    @pl.when(has_diag)
    def _():
        diag.start()
        far.start()

    @pl.when(gives_mask)
    def _():
        mask_diag.start()
        mask_far.start()

    def pair_copies(head):
        column = pl.ds(pl.multiple_of(((1 - y) * half_heads + head) * HD, HD), HD)
        return [
            remote(k_hbm.at[:, column], kv.at[1 + y, head, 0], ysend.at[head, 0],
                   kv_sem.at[1 + y, head], to_pair),
            remote(v_hbm.at[:, column], kv.at[1 + y, head, 1], ysend.at[head, 1],
                   kv_sem.at[1 + y, head], to_pair),
            remote(q_hbm.at[:, column], qs.at[y, head], ysend.at[head, 2],
                   q_sem.at[y, head], to_pair),
        ]

    def own_rows(step):
        return pl.ds(pl.multiple_of(core * width + x * part + step * piece, piece), piece)

    def wt_rows(side, step):
        return pl.ds(pl.multiple_of(side * part + step * piece, piece), piece)

    def wt_part(tile, side):
        return wt.at[tile, pl.ds(pl.multiple_of(side * part, part), part)]

    def own_weight_copies(step):
        src = w_hbm.at[own_rows(step)]
        dst = wt.at[me, wt_rows(x, step)]
        recv = w_recv.at[me, step]
        return (
            remote(src, dst, w_y, recv, to_pair),
            remote(src, dst, w_up.at[me], recv, to_up),
            remote(src, dst, w_down.at[me], recv, to_down),
        )

    own_weight = pltpu.make_async_copy(
        w_hbm.at[pl.ds(pl.multiple_of(core * width, width), width)], wt.at[me], w_own)

    @pl.loop(0, half_heads)
    def _(head):
        for copy in pair_copies(head):
            copy.start()

        for step in range(CHUNKS):
            @pl.when(head == OWN_WEIGHT_AFTER[step])
            def _():
                own_weight_copies(step)[0].start()

    @pl.loop(0, CHUNKS)
    def _(step):
        _, up, down = own_weight_copies(step)

        @pl.when(has_up)
        def _():
            up.start()

        @pl.when(has_down)
        def _():
            down.start()

    pltpu.make_async_copy(order_hbm, ordv.at[1 + y], ord_recv.at[1 + y]).start()
    pltpu.make_async_copy(mask_hbm, maskv.at[y], mask_recv.at[y]).start()

    @pl.loop(0, half_heads)
    def _(head):
        column = pl.ds(pl.multiple_of((y * half_heads + head) * HD, HD), HD)
        pltpu.make_async_copy(k_hbm.at[:, column], kv.at[1 + y, head, 0], kv_sem.at[1 + y, head]).start()
        pltpu.make_async_copy(v_hbm.at[:, column], kv.at[1 + y, head, 1], kv_sem.at[1 + y, head]).start()
        pltpu.make_async_copy(q_hbm.at[:, column], qs.at[y, head], q_sem.at[y, head]).start()

    own_weight.start()

    @pl.when(bottom)
    def _():
        ordv[0] = lax.broadcasted_iota(jnp.int32, (1, slab), 1)

    @pl.when(top)
    def _():
        ordv[3] = lax.broadcasted_iota(jnp.int32, (1, slab), 1)

    @pl.when(has_down)
    def _():
        landed(ordv.at[0], ord_recv.at[0])

    @pl.when(has_up)
    def _():
        landed(ordv.at[3], ord_recv.at[3])

    for slot in (1, 2):
        landed(ordv.at[slot], ord_recv.at[slot])
        landed(maskv.at[slot - 1], mask_recv.at[slot - 1])
    token = lax.broadcasted_iota(jnp.int32, (slab, HD), 0)
    lane = lax.broadcasted_iota(jnp.int32, (slab, HD), 1)
    tile_tok = slab // tiles
    member = jnp.where(lax.div(token, tile_tok) == lane, 1.0, 0.0).astype(jnp.bfloat16)

    @pl.loop(0, 4)
    def _(slot):
        places = ordv[slot]

        @pl.loop(0, slab // HD)
        def _(block):
            row = lax.broadcasted_iota(jnp.int32, (HD, slab), 0) + block * HD
            match = jnp.where(places == row, 1.0, 0.0).astype(jnp.bfloat16)
            hot[slot, pl.ds(pl.multiple_of(block * HD, HD), HD), :] = jnp.dot(
                match, member, preferred_element_type=jnp.float32
            ).astype(jnp.bfloat16)

    tile_row = lax.broadcasted_iota(jnp.int32, (tiles, HD), 0)
    tile_lane = lax.broadcasted_iota(jnp.int32, (tiles, HD), 1)
    row_diff = lax.div(tile_lane, GW) - lax.div(tile_row, GW)
    col_diff = lax.rem(tile_lane, GW) - lax.rem(tile_row, GW)
    near_tiles = (jnp.abs(row_diff) <= 1) & (jnp.abs(col_diff) <= 1) & (tile_lane < tiles)
    place = (row_diff + 1) * 3 + col_diff + 1

    def mask_rows(slot):
        return jnp.concatenate([maskv[slot, tile] for tile in range(tiles)], axis=0)

    def bias_of(mask, shift):
        picked = jnp.zeros((tiles, HD), jnp.int32)
        for index in range(9):
            slot = shift * 9 + index
            picked = jnp.where(place == index, mask[:, slot : slot + 1], picked)
        return jnp.where(near_tiles & (picked == 1), 0.0, HIDDEN)

    def bias_rows(slot, bias):
        bias = jnp.concatenate([bias, jnp.zeros((HD - tiles, HD), jnp.float32)], axis=0)
        return jnp.dot(
            hot[slot], bias.astype(jnp.bfloat16), preferred_element_type=jnp.float32
        ).astype(jnp.bfloat16)

    for side in range(2):
        mask = mask_rows(side)
        for shift in range(3):
            qb[side, shift] = bias_rows(1 + side, bias_of(mask, shift))

    @pl.when(helps)
    def _():
        landed(maskv.at[2], mask_recv.at[2])
        mask = mask_rows(2)
        bias = jnp.where(helps_top, bias_of(mask, 0), bias_of(mask, 2))
        qbx[...] = bias_rows(jnp.where(helps_top, 3, 0), bias)

    def neighbour_copies(head):
        up = remote(kv.at[2, head], kv.at[0, head], zsend.at[0, head], kv_sem.at[0, head], to_up)
        down = remote(kv.at[1, head], kv.at[3, head], zsend.at[1, head], kv_sem.at[3, head], to_down)
        return up, down

    def query_copies(head):
        def one(device):
            return remote(qs.at[merged, head], qx.at[head], qx_send.at[head], qx_recv.at[head], device)

        return one(to_up), one(to_down)

    def partial_copies(head):
        def one(device):
            return (
                remote(sx.at[head], ox.at[head], ox_send.at[head], ox_recv.at[head], device),
                remote(sl.at[head], lx.at[head], lx_send.at[head], lx_recv.at[head], device),
            )

        return one(to_up), one(to_down)

    def pass_on(head):
        landed(kv.at[1, head], kv_sem.at[1, head])
        landed(kv.at[2, head], kv_sem.at[2, head])
        up, down = neighbour_copies(head)

        @pl.when(has_up & jnp.logical_not(helps_top))
        def _():
            up.start()

        @pl.when(has_down & jnp.logical_not(helps_bottom))
        def _():
            down.start()

        landed(qs.at[0, head], q_sem.at[0, head])
        landed(qs.at[1, head], q_sem.at[1, head])
        up, down = query_copies(head)

        @pl.when(bottom)
        def _():
            up.start()

        @pl.when(top)
        def _():
            down.start()

    def weight_copies(tile, step):
        ref = wt.at[tile, wt_rows(x, step)]
        return (
            remote(ref, ref, w_up.at[tile], w_recv.at[tile, step], to_up),
            remote(ref, ref, w_down.at[tile], w_recv.at[tile, step], to_down),
            remote(ref, ref, w_x.at[tile], x_recv.at[tile], to_x),
        )

    def relay(event):
        kind, step = lax.div(event, CHUNKS), lax.rem(event, CHUNKS)
        last = kind == 2 * planes - 2
        other = jnp.where(last, 1, lax.rem(kind, 2))
        distance = jnp.where(last, planes - 1, lax.div(kind, 2) + 1 - other)

        @pl.loop(0, 2)
        def _(way):
            plane = z + (2 * way - 1) * distance
            valid = (plane >= 0) & (plane < planes) & ((distance > 0) | (way == 0))

            @pl.when(valid)
            def _():
                tile = 2 * plane + y + other * (1 - 2 * y)
                landed(wt.at[tile, wt_rows(x, step)], w_recv.at[tile, step])
                up, down, across = weight_copies(tile, step)

                @pl.when((plane <= z) & has_up)
                def _():
                    up.start()

                @pl.when((plane >= z) & has_down)
                def _():
                    down.start()

                across.start()

    dims = (((1,), (1,)), ((), ()))
    ones = jnp.ones((slab, HD), jnp.bfloat16)

    def attend_rows(queries, biases, blocks, head):
        peak = total = None
        for bias, block in zip(biases, blocks):
            score = lax.dot_general(
                jnp.concatenate([queries, bias], axis=1),
                jnp.concatenate([kv[block, head, 0], hot[block]], axis=1),
                dims,
                preferred_element_type=jnp.float32,
            )
            before, peak = peak, jnp.max(score, axis=1, keepdims=True)
            if before is not None:
                peak = jnp.maximum(before, peak)
            part_sum = jnp.dot(
                jnp.exp2((score - peak) * factor).astype(jnp.bfloat16),
                jnp.concatenate([kv[block, head, 1], ones], axis=1),
                preferred_element_type=jnp.float32,
            )
            total = part_sum if before is None else total * jnp.exp2((before - peak) * factor) + part_sum
        denom = total[:, HD:]
        return total[:, :HD] / denom, peak * factor + jnp.log2(denom)

    def over_rows(action):
        @pl.loop(0, slab // ROWS)
        def _(block):
            action(pl.ds(pl.multiple_of(block * ROWS, ROWS), ROWS))

    def store(head, side, rows, value):
        value = value.astype(jnp.bfloat16)

        @pl.when(side == y)
        def _():
            att[rows, pl.ds(pl.multiple_of((y * half_heads + head) * HD, HD), HD)] = value

        @pl.when(side != y)
        def _():
            snd[head, rows, :] = value

    def attend_inner(head, side):
        def action(rows):
            biases = [qb[side, shift, rows, :] for shift in range(3)]
            blocks = [side + shift for shift in range(3)]
            value, _ = attend_rows(qs[side, head, rows, :], biases, blocks, head)
            store(head, side, rows, value)

        over_rows(action)

    def attend_end(head, side, merge):
        def action(rows):
            biases = [qb[side, index + 1 - side, rows, :] for index in range(2)]
            value, level = attend_rows(qs[side, head, rows, :], biases, (1, 2), head)
            if merge:
                other = jnp.broadcast_to(lx[head, 0:1, rows], (HD, ROWS)).T
                high = jnp.maximum(level, other)
                mine, theirs = jnp.exp2(level - high), jnp.exp2(other - high)
                value = (value * mine + ox[head, rows, :].astype(jnp.float32) * theirs) / (mine + theirs)
            store(head, side, rows, value)

        over_rows(action)

    def attend_for_end(head):
        block = jnp.where(helps_top, 2, 1)

        def action(rows):
            value, level = attend_rows(qx[head, rows, :], [qbx[rows, :]], (block,), head)
            sx[head, rows, :] = value.astype(jnp.bfloat16)
            sl[head, :, rows] = level.T[:8, :]

        over_rows(action)

    def result_copy(head):
        column = pl.ds(pl.multiple_of((y * half_heads + head) * HD, HD), HD)
        return remote(snd.at[head], att.at[:, column], a_send.at[head], a_recv.at[head], to_pair)

    def relays_before(point):
        return sum(jnp.where(point > index, many, 0) for index, many in enumerate(RELAYS))

    def relays_at(point):
        @pl.loop(relays_before(point), relays_before(point + 1))
        def _(event):
            relay(event)

    pass_on(0)
    relays_at(0)

    @pl.loop(0, half_heads)
    def _(head):
        @pl.when(head + 1 < half_heads)
        def _():
            pass_on(head + 1)

        @pl.when(helps)
        def _():
            landed(qx.at[head], qx_recv.at[head])
            attend_for_end(head)
            up, down = partial_copies(head)

            @pl.when(helps_top)
            def _():
                for copy in up:
                    copy.start()

            @pl.when(helps_bottom)
            def _():
                for copy in down:
                    copy.start()

        @pl.when(jnp.logical_not(is_end))
        def _():
            landed(kv.at[0, head], kv_sem.at[0, head])
            landed(kv.at[3, head], kv_sem.at[3, head])

        @pl.loop(0, 2)
        def _(turn):
            side = jnp.where(is_end, jnp.where(turn == 0, 1 - merged, merged), jnp.where(turn == 0, 1 - y, y))

            @pl.when(jnp.logical_not(is_end))
            def _():
                attend_inner(head, side)

            @pl.when(is_end & (turn == 0))
            def _():
                attend_end(head, side, False)

            @pl.when(is_end & (turn == 1))
            def _():
                landed(ox.at[head], ox_recv.at[head])
                landed(lx.at[head], lx_recv.at[head])
                attend_end(head, side, True)

            @pl.when(side != y)
            def _():
                result_copy(head).start()

            relays_at(1 + 2 * head + turn)

    done = sum(RELAYS)

    near.wait_send()
    mask_copy.wait_send()

    @pl.when(gives_mask)
    def _():
        mask_diag.wait_send()
        mask_far.wait_send()

    @pl.when(has_diag)
    def _():
        diag.wait_send()
        far.wait_send()

    @pl.loop(0, half_heads)
    def _(head):
        for copy in pair_copies(head):
            copy.wait_send()
        up, down = neighbour_copies(head)

        @pl.when(has_up & jnp.logical_not(helps_top))
        def _():
            up.wait_send()

        @pl.when(has_down & jnp.logical_not(helps_bottom))
        def _():
            down.wait_send()

        @pl.when(is_end)
        def _():
            query_copies(head)[0].wait_send()

        @pl.when(helps)
        def _():
            for copy in partial_copies(head)[0]:
                copy.wait_send()

    def left(ref, sem):
        remote(ref, ref, sem, x_recv.at[me], to_x).wait_send()

    left(wt_part(me, x), w_y)

    def sent_results():
        @pl.loop(0, half_heads)
        def _(head):
            result_copy(head).wait_send()

    def sent_weights():
        @pl.loop(0, count)
        def _(tile):
            plane = lax.div(tile, 2)

            @pl.when((plane <= z) & has_up)
            def _():
                left(wt_part(tile, x), w_up.at[tile])

            @pl.when((plane >= z) & has_down)
            def _():
                left(wt_part(tile, x), w_down.at[tile])

            @pl.when(tile != me)
            def _():
                left(wt_part(tile, x), w_x.at[tile])


    late = half_heads - LATE

    def results_landed(first, end):
        @pl.loop(first, end)
        def _(head):
            column = pl.ds(pl.multiple_of(((1 - y) * half_heads + head) * HD, HD), HD)
            landed(att.at[:, column], a_recv.at[head])

    results_landed(0, late)
    landed(wt.at[me], w_own)

    def partial_copy(tile):
        return remote(ps.at[tile], pr.at[tile], p_send.at[tile], p_recv.at[tile], to_core)

    def out_copy(plane):
        column = pl.ds(pl.multiple_of(plane * 2 * cols, 2 * cols), 2 * cols)
        return pltpu.make_async_copy(ob.at[plane], out_hbm.at[:, column], o_sem.at[plane])

    def span(start, many):
        return pl.ds(pl.multiple_of(start * HD, HD), many * HD)

    def product(rows, tile, depth):
        return jnp.dot(att[rows, depth], wt[tile, depth, :], preferred_element_type=jnp.float32)

    own_span = span(y * half_heads, half_heads)
    early_span = span((1 - y) * half_heads, late)
    late_span = span((1 - y) * half_heads + late, LATE)
    given = pl.ds(pl.multiple_of((1 - core) * half, half), half)
    kept = pl.ds(pl.multiple_of(core * half, half), half)

    def project_early(plane):
        @pl.loop(0, 2)
        def _(which):
            tile = 2 * plane + which

            @pl.when(tile != me)
            def _():
                landed(wt_part(tile, 1 - x), x_recv.at[tile])

            ps[tile] = product(given, tile, own_span) + product(given, tile, early_span)
            po[tile] = product(kept, tile, own_span) + product(kept, tile, early_span)

    def project_late(plane):
        @pl.loop(0, 2)
        def _(which):
            tile = 2 * plane + which
            ps[tile] += product(given, tile, late_span)
            partial_copy(tile).start()

    def finish(plane):
        for which in range(2):
            tile = 2 * plane + which
            landed(pr.at[tile], p_recv.at[tile])
            total = po[tile] + product(kept, tile, late_span) + pr[tile]
            ob[plane, :, which * cols : (which + 1) * cols] = total.astype(jnp.bfloat16)
        out_copy(plane).start()

    def at_distance(distance, action):
        @pl.loop(0, 2)
        def _(way):
            plane = z + (2 * way - 1) * distance
            valid = (plane >= 0) & (plane < planes) & ((distance > 0) | (way == 0))

            @pl.when(valid)
            def _():
                action(plane)

    events = (2 * planes - 1) * CHUNKS

    def relay_for(distance):
        @pl.loop(0, 2 * CHUNKS)
        def _(index):
            event = (2 * distance + 2) * CHUNKS + index

            @pl.when((event >= done) & (event < events))
            def _():
                relay(event)

    @pl.loop(0, EARLY_DISTANCE + 1)
    def _(distance):
        relay_for(distance)
        at_distance(distance, project_early)

    results_landed(late, half_heads)

    @pl.loop(0, EARLY_DISTANCE + 1)
    def _(distance):
        at_distance(distance, project_late)

    @pl.loop(0, EARLY_DISTANCE)
    def _(distance):
        at_distance(distance, finish)

    @pl.loop(EARLY_DISTANCE + 1, planes)
    def _(distance):
        relay_for(distance)
        at_distance(distance, project_early)
        at_distance(distance, project_late)
        at_distance(distance - 1, finish)

    at_distance(planes - 1, finish)

    sent_results()
    sent_weights()

    @pl.loop(0, count)
    def _(tile):
        partial_copy(tile).wait_send()

    @pl.loop(0, planes)
    def _(plane):
        out_copy(plane).wait()


def on_device(query, key, value, tile_mask, order, out_weight):
    slab, width = query.shape
    tiles = tile_mask.shape[1]
    heads = width // HD
    count = lax.axis_size("tm")
    cols = out_weight.shape[1]
    half_heads = heads // 2
    planes = count // 2
    half = slab // 2
    bf16, f32 = jnp.bfloat16, jnp.float32
    dma = pltpu.SemaphoreType.DMA
    scratch = [
        pltpu.VMEM((4, half_heads, 2, slab, HD), bf16),
        pltpu.VMEM((2, half_heads, slab, HD), bf16),
        pltpu.VMEM((4, slab, HD), bf16),
        pltpu.VMEM((2, 3, slab, HD), bf16),
        pltpu.VMEM((4, 1, slab), jnp.int32),
        pltpu.VMEM((3, tiles, 1, tile_mask.shape[2]), jnp.int32),
        pltpu.VMEM((count, width, cols), bf16),
        pltpu.VMEM((slab, width), bf16),
        pltpu.VMEM((half_heads, slab, HD), bf16),
        pltpu.VMEM((half_heads, slab, HD), bf16),
        pltpu.VMEM((slab, HD), bf16),
        pltpu.VMEM((half_heads, slab, HD), bf16),
        pltpu.VMEM((half_heads, 8, slab), f32),
        pltpu.VMEM((half_heads, slab, HD), bf16),
        pltpu.VMEM((half_heads, 8, slab), f32),
        pltpu.VMEM((count, half, cols), f32),
        pltpu.VMEM((count, half, cols), f32),
        pltpu.VMEM((count, half, cols), f32),
        pltpu.VMEM((planes, half, 2 * cols), bf16),
        dma((4, half_heads)),
        dma((2, half_heads)),
        dma((half_heads, 3)),
        dma((2, half_heads)),
        dma((4,)),
        dma((3,)),
        dma((3,)),
        dma((3,)),
        dma((count, CHUNKS)),
        dma((count,)),
        dma((count,)),
        dma((count,)),
        dma((count,)),
        dma,
        dma,
        dma((half_heads,)),
        dma((half_heads,)),
        dma((count,)),
        dma((count,)),
        dma((planes,)),
        dma((half_heads,)),
        dma((half_heads,)),
        dma((half_heads,)),
        dma((half_heads,)),
        dma((half_heads,)),
        dma((half_heads,)),
    ]
    sizes = (count, heads, slab, tiles, width, cols)
    return pl.pallas_call(
        functools.partial(kernel, sizes),
        in_specs=[pl.BlockSpec(memory_space=pltpu.HBM)] * 6,
        out_specs=pl.BlockSpec(memory_space=pltpu.HBM),
        out_shape=jax.ShapeDtypeStruct((half, count * cols), bf16),
        scratch_shapes=scratch,
        compiler_params=pltpu.CompilerParams(
            collective_id=0, has_side_effects=True, vmem_limit_bytes=60 << 20
        ),
        cost_estimate=pl.CostEstimate(
            flops=4 * heads * slab * 3 * slab * HD + 2 * slab * width * count * cols,
            bytes_accessed=8 * slab * width,
            transcendentals=heads * slab * 3 * slab,
        ),
        name="clip_attention",
    )(query, key, value, tile_mask.transpose(1, 0, 2), order, out_weight)


def solution(mesh):
    placed = (
        P(("clips", "tm"), "head"),
        P(("clips", "tm"), "head"),
        P(("clips", "tm"), "head"),
        P(("clips", "tm"), None, None),
        P(("clips", "tm"), None),
        P(None, "tm"),
    )
    return jax.shard_map(
        on_device,
        mesh=mesh,
        in_specs=placed,
        out_specs=P(("clips", "tm", "head"), None),
        check_vma=False,
    )
```

```python
import functools
import math

import jax
import jax.numpy as jnp
from jax import lax
from jax.experimental import pallas as pl
from jax.experimental.pallas import tpu as pltpu
from jax.sharding import PartitionSpec as P

HD = 128
GW = 3
HIDDEN = -1e30
CHUNKS = 3
ROWS = 768
LATE = 2
EARLY_DISTANCE = 2
OWN_WEIGHT_AFTER = (0, 0, 1)
RELAYS = (5, 3, 0, 0, 2, 5, 0, 2, 0, 4, 0, 0, 0)
MESH = pl.DeviceIdType.MESH


def kernel(sizes, q_hbm, k_hbm, v_hbm, mask_hbm, order_hbm, w_hbm, out_ref, *scratch):
    count, heads, slab, tiles, width, cols = sizes
    (kv, qs, hot, qb, ordv, maskv, wt, att, snd, qx, qbx, ox, lx, sx, sl, ps, pb, pr, po, ob,
     kv_sem, q_sem, ysend, zsend, ord_recv, ord_send, mask_recv, mask_send,
     w_recv, x_recv, w_up, w_down, w_x, w_y, w_own,
     a_recv, a_send, p_recv, p_send, o_sem,
     qx_recv, qx_send, ox_recv, ox_send, lx_recv, lx_send) = scratch
    half_heads = heads // 2
    planes = count // 2
    part = width // 2
    piece = part // CHUNKS
    half = slab // 2
    aligned = cols % HD == 0
    factor = HD ** (-0.5) * math.log2(math.e)

    clip = lax.axis_index("clips")
    me = lax.axis_index("tm")
    core = lax.axis_index("head")
    x = lax.rem(clip, 2)
    z = lax.div(me, 2)
    y = lax.rem(me, 2)
    pair = me + 1 - 2 * y
    sign = 2 * y - 1
    has_up = z < planes - 1
    has_down = z > 0
    has_diag = (z + sign >= 0) & (z + sign < planes)
    top, bottom = z == planes - 1, z == 0
    is_end = top | bottom
    helps_top, helps_bottom = z == planes - 2, z == 1
    helps = helps_top | helps_bottom
    merged = jnp.where(top, 0, 1)

    to_pair = (clip, pair, core)
    to_up = (clip, me + 2, core)
    to_down = (clip, me - 2, core)
    to_diag = (clip, me + sign, core)
    to_far = (clip, me + 2 * sign, core)
    to_x = (clip + 1 - 2 * x, me, core)
    to_core = (clip, me, 1 - core)

    def remote(src, dst, send, recv, device):
        return pltpu.make_async_remote_copy(
            src_ref=src, dst_ref=dst, send_sem=send, recv_sem=recv,
            device_id=device, device_id_type=MESH,
        )

    def landed(ref, sem):
        pltpu.make_async_copy(ref, ref, sem).wait()

    barrier = pltpu.get_barrier_semaphore()
    for device in (to_pair, to_x, to_core):
        pl.semaphore_signal(barrier, inc=1, device_id=device, device_id_type=MESH)
    for device, valid in ((to_up, has_up), (to_down, has_down), (to_diag, has_diag)):
        @pl.when(valid)
        def _():
            pl.semaphore_signal(barrier, inc=1, device_id=device, device_id_type=MESH)
    pl.semaphore_wait(
        barrier,
        3 + has_up.astype(jnp.int32) + has_down.astype(jnp.int32) + has_diag.astype(jnp.int32),
    )

    def order_copies():
        near = remote(order_hbm, ordv.at[1 + y], ord_send.at[0], ord_recv.at[1 + y], to_pair)
        slot = 3 - 3 * y
        diag = remote(order_hbm, ordv.at[slot], ord_send.at[1], ord_recv.at[slot], to_diag)
        far = remote(order_hbm, ordv.at[slot], ord_send.at[2], ord_recv.at[slot], to_far)
        return near, diag, far

    mask_copy = remote(mask_hbm, maskv.at[y], mask_send.at[0], mask_recv.at[y], to_pair)
    mask_diag = remote(mask_hbm, maskv.at[2], mask_send.at[1], mask_recv.at[2], to_diag)
    mask_far = remote(mask_hbm, maskv.at[2], mask_send.at[2], mask_recv.at[2], to_far)
    gives_mask = is_end & has_diag
    near, diag, far = order_copies()
    near.start()
    mask_copy.start()

    @pl.when(has_diag)
    def _():
        diag.start()
        far.start()

    @pl.when(gives_mask)
    def _():
        mask_diag.start()
        mask_far.start()

    def pair_copies(head):
        column = pl.ds(pl.multiple_of(((1 - y) * half_heads + head) * HD, HD), HD)
        return [
            remote(k_hbm.at[:, column], kv.at[1 + y, head, 0], ysend.at[head, 0],
                   kv_sem.at[1 + y, head], to_pair),
            remote(v_hbm.at[:, column], kv.at[1 + y, head, 1], ysend.at[head, 1],
                   kv_sem.at[1 + y, head], to_pair),
            remote(q_hbm.at[:, column], qs.at[y, head], ysend.at[head, 2],
                   q_sem.at[y, head], to_pair),
        ]

    def own_rows(step):
        return pl.ds(pl.multiple_of(core * width + x * part + step * piece, piece), piece)

    def wt_rows(side, step):
        return pl.ds(pl.multiple_of(side * part + step * piece, piece), piece)

    def wt_part(tile, side):
        return wt.at[tile, pl.ds(pl.multiple_of(side * part, part), part)]

    def own_weight_copies(step):
        src = w_hbm.at[own_rows(step)]
        dst = wt.at[me, wt_rows(x, step)]
        recv = w_recv.at[me, step]
        return (
            remote(src, dst, w_y, recv, to_pair),
            remote(src, dst, w_up.at[me], recv, to_up),
            remote(src, dst, w_down.at[me], recv, to_down),
        )

    own_weight = pltpu.make_async_copy(
        w_hbm.at[pl.ds(pl.multiple_of(core * width, width), width)], wt.at[me], w_own)

    @pl.loop(0, half_heads)
    def _(head):
        for copy in pair_copies(head):
            copy.start()

        for step in range(CHUNKS):
            @pl.when(head == OWN_WEIGHT_AFTER[step])
            def _():
                own_weight_copies(step)[0].start()

    @pl.loop(0, CHUNKS)
    def _(step):
        _, up, down = own_weight_copies(step)

        @pl.when(has_up)
        def _():
            up.start()

        @pl.when(has_down)
        def _():
            down.start()

    pltpu.make_async_copy(order_hbm, ordv.at[1 + y], ord_recv.at[1 + y]).start()
    pltpu.make_async_copy(mask_hbm, maskv.at[y], mask_recv.at[y]).start()

    @pl.loop(0, half_heads)
    def _(head):
        column = pl.ds(pl.multiple_of((y * half_heads + head) * HD, HD), HD)
        pltpu.make_async_copy(k_hbm.at[:, column], kv.at[1 + y, head, 0], kv_sem.at[1 + y, head]).start()
        pltpu.make_async_copy(v_hbm.at[:, column], kv.at[1 + y, head, 1], kv_sem.at[1 + y, head]).start()
        pltpu.make_async_copy(q_hbm.at[:, column], qs.at[y, head], q_sem.at[y, head]).start()

    own_weight.start()

    @pl.when(bottom)
    def _():
        ordv[0] = lax.broadcasted_iota(jnp.int32, (1, slab), 1)

    @pl.when(top)
    def _():
        ordv[3] = lax.broadcasted_iota(jnp.int32, (1, slab), 1)

    @pl.when(has_down)
    def _():
        landed(ordv.at[0], ord_recv.at[0])

    @pl.when(has_up)
    def _():
        landed(ordv.at[3], ord_recv.at[3])

    for slot in (1, 2):
        landed(ordv.at[slot], ord_recv.at[slot])
        landed(maskv.at[slot - 1], mask_recv.at[slot - 1])
    token = lax.broadcasted_iota(jnp.int32, (slab, HD), 0)
    lane = lax.broadcasted_iota(jnp.int32, (slab, HD), 1)
    tile_tok = slab // tiles
    member = jnp.where(lax.div(token, tile_tok) == lane, 1.0, 0.0).astype(jnp.bfloat16)

    @pl.loop(0, 4)
    def _(slot):
        places = ordv[slot]

        @pl.loop(0, slab // HD)
        def _(block):
            row = lax.broadcasted_iota(jnp.int32, (HD, slab), 0) + block * HD
            match = jnp.where(places == row, 1.0, 0.0).astype(jnp.bfloat16)
            hot[slot, pl.ds(pl.multiple_of(block * HD, HD), HD), :] = jnp.dot(
                match, member, preferred_element_type=jnp.float32
            ).astype(jnp.bfloat16)

    tile_row = lax.broadcasted_iota(jnp.int32, (tiles, HD), 0)
    tile_lane = lax.broadcasted_iota(jnp.int32, (tiles, HD), 1)
    row_diff = lax.div(tile_lane, GW) - lax.div(tile_row, GW)
    col_diff = lax.rem(tile_lane, GW) - lax.rem(tile_row, GW)
    near_tiles = (jnp.abs(row_diff) <= 1) & (jnp.abs(col_diff) <= 1) & (tile_lane < tiles)
    place = (row_diff + 1) * 3 + col_diff + 1

    def mask_rows(slot):
        return jnp.concatenate([maskv[slot, tile] for tile in range(tiles)], axis=0)

    def bias_of(mask, shift):
        picked = jnp.zeros((tiles, HD), jnp.int32)
        for index in range(9):
            slot = shift * 9 + index
            picked = jnp.where(place == index, mask[:, slot : slot + 1], picked)
        return jnp.where(near_tiles & (picked == 1), 0.0, HIDDEN)

    def bias_rows(slot, bias):
        bias = jnp.concatenate([bias, jnp.zeros((HD - tiles, HD), jnp.float32)], axis=0)
        return jnp.dot(
            hot[slot], bias.astype(jnp.bfloat16), preferred_element_type=jnp.float32
        ).astype(jnp.bfloat16)

    for side in range(2):
        mask = mask_rows(side)
        for shift in range(3):
            qb[side, shift] = bias_rows(1 + side, bias_of(mask, shift))

    @pl.when(helps)
    def _():
        landed(maskv.at[2], mask_recv.at[2])
        mask = mask_rows(2)
        bias = jnp.where(helps_top, bias_of(mask, 0), bias_of(mask, 2))
        qbx[...] = bias_rows(jnp.where(helps_top, 3, 0), bias)

    def neighbour_copies(head):
        up = remote(kv.at[2, head], kv.at[0, head], zsend.at[0, head], kv_sem.at[0, head], to_up)
        down = remote(kv.at[1, head], kv.at[3, head], zsend.at[1, head], kv_sem.at[3, head], to_down)
        return up, down

    def query_copies(head):
        def one(device):
            return remote(qs.at[merged, head], qx.at[head], qx_send.at[head], qx_recv.at[head], device)

        return one(to_up), one(to_down)

    def partial_copies(head):
        def one(device):
            return (
                remote(sx.at[head], ox.at[head], ox_send.at[head], ox_recv.at[head], device),
                remote(sl.at[head], lx.at[head], lx_send.at[head], lx_recv.at[head], device),
            )

        return one(to_up), one(to_down)

    def pass_on(head):
        landed(kv.at[1, head], kv_sem.at[1, head])
        landed(kv.at[2, head], kv_sem.at[2, head])
        up, down = neighbour_copies(head)

        @pl.when(has_up & jnp.logical_not(helps_top))
        def _():
            up.start()

        @pl.when(has_down & jnp.logical_not(helps_bottom))
        def _():
            down.start()

        landed(qs.at[0, head], q_sem.at[0, head])
        landed(qs.at[1, head], q_sem.at[1, head])
        up, down = query_copies(head)

        @pl.when(bottom)
        def _():
            up.start()

        @pl.when(top)
        def _():
            down.start()

    def weight_copies(tile, step):
        ref = wt.at[tile, wt_rows(x, step)]
        return (
            remote(ref, ref, w_up.at[tile], w_recv.at[tile, step], to_up),
            remote(ref, ref, w_down.at[tile], w_recv.at[tile, step], to_down),
            remote(ref, ref, w_x.at[tile], x_recv.at[tile], to_x),
        )

    def relay(event):
        kind, step = lax.div(event, CHUNKS), lax.rem(event, CHUNKS)
        last = kind == 2 * planes - 2
        other = jnp.where(last, 1, lax.rem(kind, 2))
        distance = jnp.where(last, planes - 1, lax.div(kind, 2) + 1 - other)

        @pl.loop(0, 2)
        def _(way):
            plane = z + (2 * way - 1) * distance
            valid = (plane >= 0) & (plane < planes) & ((distance > 0) | (way == 0))

            @pl.when(valid)
            def _():
                tile = 2 * plane + y + other * (1 - 2 * y)
                landed(wt.at[tile, wt_rows(x, step)], w_recv.at[tile, step])
                up, down, across = weight_copies(tile, step)

                @pl.when((plane <= z) & has_up)
                def _():
                    up.start()

                @pl.when((plane >= z) & has_down)
                def _():
                    down.start()

                across.start()

    dims = (((1,), (1,)), ((), ()))
    ones = jnp.ones((slab, HD), jnp.bfloat16)

    def attend_rows(queries, biases, blocks, head):
        peak = total = None
        for bias, block in zip(biases, blocks):
            score = lax.dot_general(
                jnp.concatenate([queries, bias], axis=1),
                jnp.concatenate([kv[block, head, 0], hot[block]], axis=1),
                dims,
                preferred_element_type=jnp.float32,
            )
            before, peak = peak, jnp.max(score, axis=1, keepdims=True)
            if before is not None:
                peak = jnp.maximum(before, peak)
            part_sum = jnp.dot(
                jnp.exp2((score - peak) * factor).astype(jnp.bfloat16),
                jnp.concatenate([kv[block, head, 1], ones], axis=1),
                preferred_element_type=jnp.float32,
            )
            total = part_sum if before is None else total * jnp.exp2((before - peak) * factor) + part_sum
        denom = total[:, HD:]
        return total[:, :HD] / denom, peak * factor + jnp.log2(denom)

    def over_rows(action):
        @pl.loop(0, slab // ROWS)
        def _(block):
            action(pl.ds(pl.multiple_of(block * ROWS, ROWS), ROWS))

    def store(head, side, rows, value):
        value = value.astype(jnp.bfloat16)

        @pl.when(side == y)
        def _():
            att[rows, pl.ds(pl.multiple_of((y * half_heads + head) * HD, HD), HD)] = value

        @pl.when(side != y)
        def _():
            snd[head, rows, :] = value

    def attend_inner(head, side):
        def action(rows):
            biases = [qb[side, shift, rows, :] for shift in range(3)]
            blocks = [side + shift for shift in range(3)]
            value, _ = attend_rows(qs[side, head, rows, :], biases, blocks, head)
            store(head, side, rows, value)

        over_rows(action)

    def attend_end(head, side, merge):
        def action(rows):
            biases = [qb[side, index + 1 - side, rows, :] for index in range(2)]
            value, level = attend_rows(qs[side, head, rows, :], biases, (1, 2), head)
            if merge:
                other = jnp.broadcast_to(lx[head, 0:1, rows], (HD, ROWS)).T
                high = jnp.maximum(level, other)
                mine, theirs = jnp.exp2(level - high), jnp.exp2(other - high)
                value = (value * mine + ox[head, rows, :].astype(jnp.float32) * theirs) / (mine + theirs)
            store(head, side, rows, value)

        over_rows(action)

    def attend_for_end(head):
        block = jnp.where(helps_top, 2, 1)

        def action(rows):
            value, level = attend_rows(qx[head, rows, :], [qbx[rows, :]], (block,), head)
            sx[head, rows, :] = value.astype(jnp.bfloat16)
            sl[head, :, rows] = level.T[:8, :]

        over_rows(action)

    def result_copy(head):
        column = pl.ds(pl.multiple_of((y * half_heads + head) * HD, HD), HD)
        return remote(snd.at[head], att.at[:, column], a_send.at[head], a_recv.at[head], to_pair)

    def relays_before(point):
        return sum(jnp.where(point > index, many, 0) for index, many in enumerate(RELAYS))

    def relays_at(point):
        @pl.loop(relays_before(point), relays_before(point + 1))
        def _(event):
            relay(event)

    pass_on(0)
    relays_at(0)

    @pl.loop(0, half_heads)
    def _(head):
        @pl.when(head + 1 < half_heads)
        def _():
            pass_on(head + 1)

        @pl.when(helps)
        def _():
            landed(qx.at[head], qx_recv.at[head])
            attend_for_end(head)
            up, down = partial_copies(head)

            @pl.when(helps_top)
            def _():
                for copy in up:
                    copy.start()

            @pl.when(helps_bottom)
            def _():
                for copy in down:
                    copy.start()

        @pl.when(jnp.logical_not(is_end))
        def _():
            landed(kv.at[0, head], kv_sem.at[0, head])
            landed(kv.at[3, head], kv_sem.at[3, head])

        @pl.loop(0, 2)
        def _(turn):
            side = jnp.where(is_end, jnp.where(turn == 0, 1 - merged, merged), jnp.where(turn == 0, 1 - y, y))

            @pl.when(jnp.logical_not(is_end))
            def _():
                attend_inner(head, side)

            @pl.when(is_end & (turn == 0))
            def _():
                attend_end(head, side, False)

            @pl.when(is_end & (turn == 1))
            def _():
                landed(ox.at[head], ox_recv.at[head])
                landed(lx.at[head], lx_recv.at[head])
                attend_end(head, side, True)

            @pl.when(side != y)
            def _():
                result_copy(head).start()

            relays_at(1 + 2 * head + turn)

    done = sum(RELAYS)

    near.wait_send()
    mask_copy.wait_send()

    @pl.when(gives_mask)
    def _():
        mask_diag.wait_send()
        mask_far.wait_send()

    @pl.when(has_diag)
    def _():
        diag.wait_send()
        far.wait_send()

    @pl.loop(0, half_heads)
    def _(head):
        for copy in pair_copies(head):
            copy.wait_send()
        up, down = neighbour_copies(head)

        @pl.when(has_up & jnp.logical_not(helps_top))
        def _():
            up.wait_send()

        @pl.when(has_down & jnp.logical_not(helps_bottom))
        def _():
            down.wait_send()

        @pl.when(is_end)
        def _():
            query_copies(head)[0].wait_send()

        @pl.when(helps)
        def _():
            for copy in partial_copies(head)[0]:
                copy.wait_send()

    def left(ref, sem):
        remote(ref, ref, sem, x_recv.at[me], to_x).wait_send()

    left(wt_part(me, x), w_y)

    def sent_results():
        @pl.loop(0, half_heads)
        def _(head):
            result_copy(head).wait_send()

    def sent_weights():
        @pl.loop(0, count)
        def _(tile):
            plane = lax.div(tile, 2)

            @pl.when((plane <= z) & has_up)
            def _():
                left(wt_part(tile, x), w_up.at[tile])

            @pl.when((plane >= z) & has_down)
            def _():
                left(wt_part(tile, x), w_down.at[tile])

            @pl.when(tile != me)
            def _():
                left(wt_part(tile, x), w_x.at[tile])


    late = half_heads - LATE

    def results_landed(first, end):
        @pl.loop(first, end)
        def _(head):
            column = pl.ds(pl.multiple_of(((1 - y) * half_heads + head) * HD, HD), HD)
            landed(att.at[:, column], a_recv.at[head])

    results_landed(0, late)
    landed(wt.at[me], w_own)

    def partial_copy(tile):
        return remote(pb.at[tile], pr.at[tile], p_send.at[tile], p_recv.at[tile], to_core)

    def out_copy(plane):
        column = pl.ds(pl.multiple_of(plane * 2 * cols, 2 * cols), 2 * cols)
        return pltpu.make_async_copy(ob.at[plane], out_ref.at[:, column], o_sem.at[plane])

    def span(start, many):
        return pl.ds(pl.multiple_of(start * HD, HD), many * HD)

    def product(rows, tile, depth):
        return jnp.dot(att[rows, depth], wt[tile, depth, :], preferred_element_type=jnp.float32)

    own_span = span(y * half_heads, half_heads)
    early_span = span((1 - y) * half_heads, late)
    late_span = span((1 - y) * half_heads + late, LATE)
    given = pl.ds(pl.multiple_of((1 - core) * half, half), half)
    kept = pl.ds(pl.multiple_of(core * half, half), half)

    def project_early(plane):
        @pl.loop(0, 2)
        def _(which):
            tile = 2 * plane + which

            @pl.when(tile != me)
            def _():
                landed(wt_part(tile, 1 - x), x_recv.at[tile])

            ps[tile] = product(given, tile, own_span) + product(given, tile, early_span)
            po[tile] = product(kept, tile, own_span) + product(kept, tile, early_span)

    def project_late(plane):
        @pl.loop(0, 2)
        def _(which):
            tile = 2 * plane + which
            sums = ps[tile] + product(given, tile, late_span)
            pb[tile] = sums.astype(jnp.bfloat16)
            partial_copy(tile).start()

    def finish(plane):
        for which in range(2):
            tile = 2 * plane + which
            landed(pr.at[tile], p_recv.at[tile])
            total = po[tile] + product(kept, tile, late_span) + pr[tile].astype(jnp.float32)
            total = total.astype(jnp.bfloat16)
            if aligned:
                out_ref[:, pl.ds(pl.multiple_of(tile * cols, HD), cols)] = total
            else:
                ob[plane, :, which * cols : (which + 1) * cols] = total
        if not aligned:
            out_copy(plane).start()

    def at_distance(distance, action):
        @pl.loop(0, 2)
        def _(way):
            plane = z + (2 * way - 1) * distance
            valid = (plane >= 0) & (plane < planes) & ((distance > 0) | (way == 0))

            @pl.when(valid)
            def _():
                action(plane)

    events = (2 * planes - 1) * CHUNKS

    def relay_for(distance):
        @pl.loop(0, 2 * CHUNKS)
        def _(index):
            event = (2 * distance + 2) * CHUNKS + index

            @pl.when((event >= done) & (event < events))
            def _():
                relay(event)

    @pl.loop(0, EARLY_DISTANCE + 1)
    def _(distance):
        relay_for(distance)
        at_distance(distance, project_early)

    results_landed(late, half_heads)

    @pl.loop(0, EARLY_DISTANCE + 1)
    def _(distance):
        at_distance(distance, project_late)

    @pl.loop(0, EARLY_DISTANCE)
    def _(distance):
        at_distance(distance, finish)

    @pl.loop(EARLY_DISTANCE + 1, planes)
    def _(distance):
        relay_for(distance)
        at_distance(distance, project_early)
        at_distance(distance, project_late)
        at_distance(distance - 1, finish)

    at_distance(planes - 1, finish)

    sent_results()
    sent_weights()

    @pl.loop(0, count)
    def _(tile):
        partial_copy(tile).wait_send()

    if not aligned:
        @pl.loop(0, planes)
        def _(plane):
            out_copy(plane).wait()


def on_device(query, key, value, tile_mask, order, out_weight):
    slab, width = query.shape
    tiles = tile_mask.shape[1]
    heads = width // HD
    count = lax.axis_size("tm")
    cols = out_weight.shape[1]
    half_heads = heads // 2
    planes = count // 2
    half = slab // 2
    bf16, f32 = jnp.bfloat16, jnp.float32
    dma = pltpu.SemaphoreType.DMA
    scratch = [
        pltpu.VMEM((4, half_heads, 2, slab, HD), bf16),
        pltpu.VMEM((2, half_heads, slab, HD), bf16),
        pltpu.VMEM((4, slab, HD), bf16),
        pltpu.VMEM((2, 3, slab, HD), bf16),
        pltpu.VMEM((4, 1, slab), jnp.int32),
        pltpu.VMEM((3, tiles, 1, tile_mask.shape[2]), jnp.int32),
        pltpu.VMEM((count, width, cols), bf16),
        pltpu.VMEM((slab, width), bf16),
        pltpu.VMEM((half_heads, slab, HD), bf16),
        pltpu.VMEM((half_heads, slab, HD), bf16),
        pltpu.VMEM((slab, HD), bf16),
        pltpu.VMEM((half_heads, slab, HD), bf16),
        pltpu.VMEM((half_heads, 8, slab), f32),
        pltpu.VMEM((half_heads, slab, HD), bf16),
        pltpu.VMEM((half_heads, 8, slab), f32),
        pltpu.VMEM((count, half, cols), f32),
        pltpu.VMEM((count, half, cols), bf16),
        pltpu.VMEM((count, half, cols), bf16),
        pltpu.VMEM((count, half, cols), f32),
        pltpu.VMEM((planes, half, 2 * cols) if cols % HD else (8, HD), bf16),
        dma((4, half_heads)),
        dma((2, half_heads)),
        dma((half_heads, 3)),
        dma((2, half_heads)),
        dma((4,)),
        dma((3,)),
        dma((3,)),
        dma((3,)),
        dma((count, CHUNKS)),
        dma((count,)),
        dma((count,)),
        dma((count,)),
        dma((count,)),
        dma,
        dma,
        dma((half_heads,)),
        dma((half_heads,)),
        dma((count,)),
        dma((count,)),
        dma((planes,)),
        dma((half_heads,)),
        dma((half_heads,)),
        dma((half_heads,)),
        dma((half_heads,)),
        dma((half_heads,)),
        dma((half_heads,)),
    ]
    sizes = (count, heads, slab, tiles, width, cols)
    return pl.pallas_call(
        functools.partial(kernel, sizes),
        in_specs=[pl.BlockSpec(memory_space=pltpu.HBM)] * 6,
        out_specs=pl.BlockSpec(memory_space=pltpu.VMEM),
        out_shape=pltpu.VMEM((half, count * cols), bf16),
        scratch_shapes=scratch,
        compiler_params=pltpu.CompilerParams(
            collective_id=0, has_side_effects=True, vmem_limit_bytes=58 << 20
        ),
        cost_estimate=pl.CostEstimate(
            flops=4 * heads * slab * 3 * slab * HD + 2 * slab * width * count * cols,
            bytes_accessed=8 * slab * width,
            transcendentals=heads * slab * 3 * slab,
        ),
        name="clip_attention",
    )(query, key, value, tile_mask.transpose(1, 0, 2), order, out_weight)


def solution(mesh):
    placed = (
        P(("clips", "tm"), "head"),
        P(("clips", "tm"), "head"),
        P(("clips", "tm"), "head"),
        P(("clips", "tm"), None, None),
        P(("clips", "tm"), None),
        P(None, "tm"),
    )
    return jax.shard_map(
        on_device,
        mesh=mesh,
        in_specs=placed,
        out_specs=P(("clips", "tm", "head"), None),
        check_vma=False,
    )
```

```python
import functools
import math

import jax
import jax.numpy as jnp
from jax import lax
from jax.experimental import pallas as pl
from jax.experimental.pallas import tpu as pltpu
from jax.sharding import PartitionSpec as P

HD = 128
GW = 3
HIDDEN = -1e30
CHUNKS = 3
ROWS = 768
LATE = 2
EARLY_DISTANCE = 2
OWN_WEIGHT_AFTER = (0, 0, 1)
RELAYS = (5, 3, 0, 0, 2, 5, 0, 2, 0, 4, 0, 0, 0)
MESH = pl.DeviceIdType.MESH


def kernel(sizes, q_hbm, k_hbm, v_hbm, mask_hbm, order_hbm, w_hbm, out_ref, *scratch):
    count, heads, slab, tiles, width, cols = sizes
    (kv, qs, hot, qb, ordv, maskv, wt, att, snd, qx, qbx, ox, lx, sx, sl, pe, pb, pr, ob,
     kv_sem, q_sem, ysend, zsend, ord_recv, ord_send, mask_recv, mask_send,
     w_recv, x_recv, w_up, w_down, w_x, w_y, w_own,
     a_recv, a_send, p_recv, p_send, o_sem,
     qx_recv, qx_send, ox_recv, ox_send, lx_recv, lx_send) = scratch
    half_heads = heads // 2
    planes = count // 2
    part = width // 2
    piece = part // CHUNKS
    half = slab // 2
    aligned = cols % HD == 0
    factor = HD ** (-0.5) * math.log2(math.e)

    clip = lax.axis_index("clips")
    me = lax.axis_index("tm")
    core = lax.axis_index("head")
    x = lax.rem(clip, 2)
    z = lax.div(me, 2)
    y = lax.rem(me, 2)
    pair = me + 1 - 2 * y
    sign = 2 * y - 1
    has_up = z < planes - 1
    has_down = z > 0
    has_diag = (z + sign >= 0) & (z + sign < planes)
    top, bottom = z == planes - 1, z == 0
    is_end = top | bottom
    helps_top, helps_bottom = z == planes - 2, z == 1
    helps = helps_top | helps_bottom
    merged = jnp.where(top, 0, 1)

    to_pair = (clip, pair, core)
    to_up = (clip, me + 2, core)
    to_down = (clip, me - 2, core)
    to_diag = (clip, me + sign, core)
    to_far = (clip, me + 2 * sign, core)
    to_x = (clip + 1 - 2 * x, me, core)
    to_core = (clip, me, 1 - core)

    def remote(src, dst, send, recv, device):
        return pltpu.make_async_remote_copy(
            src_ref=src, dst_ref=dst, send_sem=send, recv_sem=recv,
            device_id=device, device_id_type=MESH,
        )

    def landed(ref, sem):
        pltpu.make_async_copy(ref, ref, sem).wait()

    barrier = pltpu.get_barrier_semaphore()
    for device in (to_pair, to_x, to_core):
        pl.semaphore_signal(barrier, inc=1, device_id=device, device_id_type=MESH)
    for device, valid in ((to_up, has_up), (to_down, has_down), (to_diag, has_diag)):
        @pl.when(valid)
        def _():
            pl.semaphore_signal(barrier, inc=1, device_id=device, device_id_type=MESH)
    pl.semaphore_wait(
        barrier,
        3 + has_up.astype(jnp.int32) + has_down.astype(jnp.int32) + has_diag.astype(jnp.int32),
    )

    def order_copies():
        near = remote(order_hbm, ordv.at[1 + y], ord_send.at[0], ord_recv.at[1 + y], to_pair)
        slot = 3 - 3 * y
        diag = remote(order_hbm, ordv.at[slot], ord_send.at[1], ord_recv.at[slot], to_diag)
        far = remote(order_hbm, ordv.at[slot], ord_send.at[2], ord_recv.at[slot], to_far)
        return near, diag, far

    mask_copy = remote(mask_hbm, maskv.at[y], mask_send.at[0], mask_recv.at[y], to_pair)
    mask_diag = remote(mask_hbm, maskv.at[2], mask_send.at[1], mask_recv.at[2], to_diag)
    mask_far = remote(mask_hbm, maskv.at[2], mask_send.at[2], mask_recv.at[2], to_far)
    gives_mask = is_end & has_diag
    near, diag, far = order_copies()
    near.start()
    mask_copy.start()

    @pl.when(has_diag)
    def _():
        diag.start()
        far.start()

    @pl.when(gives_mask)
    def _():
        mask_diag.start()
        mask_far.start()

    def pair_copies(head):
        column = pl.ds(pl.multiple_of(((1 - y) * half_heads + head) * HD, HD), HD)
        return [
            remote(k_hbm.at[:, column], kv.at[1 + y, head, 0], ysend.at[head, 0],
                   kv_sem.at[1 + y, head], to_pair),
            remote(v_hbm.at[:, column], kv.at[1 + y, head, 1], ysend.at[head, 1],
                   kv_sem.at[1 + y, head], to_pair),
            remote(q_hbm.at[:, column], qs.at[y, head], ysend.at[head, 2],
                   q_sem.at[y, head], to_pair),
        ]

    def own_rows(step):
        return pl.ds(pl.multiple_of(core * width + x * part + step * piece, piece), piece)

    def wt_rows(side, step):
        return pl.ds(pl.multiple_of(side * part + step * piece, piece), piece)

    def wt_part(tile, side):
        return wt.at[tile, pl.ds(pl.multiple_of(side * part, part), part)]

    def own_weight_copies(step):
        src = w_hbm.at[own_rows(step)]
        dst = wt.at[me, wt_rows(x, step)]
        recv = w_recv.at[me, step]
        return (
            remote(src, dst, w_y, recv, to_pair),
            remote(src, dst, w_up.at[me], recv, to_up),
            remote(src, dst, w_down.at[me], recv, to_down),
        )

    own_weight = pltpu.make_async_copy(
        w_hbm.at[pl.ds(pl.multiple_of(core * width, width), width)], wt.at[me], w_own)

    @pl.loop(0, half_heads)
    def _(head):
        for copy in pair_copies(head):
            copy.start()

        for step in range(CHUNKS):
            @pl.when(head == OWN_WEIGHT_AFTER[step])
            def _():
                own_weight_copies(step)[0].start()

    @pl.loop(0, CHUNKS)
    def _(step):
        _, up, down = own_weight_copies(step)

        @pl.when(has_up)
        def _():
            up.start()

        @pl.when(has_down)
        def _():
            down.start()

    pltpu.make_async_copy(order_hbm, ordv.at[1 + y], ord_recv.at[1 + y]).start()
    pltpu.make_async_copy(mask_hbm, maskv.at[y], mask_recv.at[y]).start()

    @pl.loop(0, half_heads)
    def _(head):
        column = pl.ds(pl.multiple_of((y * half_heads + head) * HD, HD), HD)
        pltpu.make_async_copy(k_hbm.at[:, column], kv.at[1 + y, head, 0], kv_sem.at[1 + y, head]).start()
        pltpu.make_async_copy(v_hbm.at[:, column], kv.at[1 + y, head, 1], kv_sem.at[1 + y, head]).start()
        pltpu.make_async_copy(q_hbm.at[:, column], qs.at[y, head], q_sem.at[y, head]).start()

    own_weight.start()

    @pl.when(bottom)
    def _():
        ordv[0] = lax.broadcasted_iota(jnp.int32, (1, slab), 1)

    @pl.when(top)
    def _():
        ordv[3] = lax.broadcasted_iota(jnp.int32, (1, slab), 1)

    @pl.when(has_down)
    def _():
        landed(ordv.at[0], ord_recv.at[0])

    @pl.when(has_up)
    def _():
        landed(ordv.at[3], ord_recv.at[3])

    for slot in (1, 2):
        landed(ordv.at[slot], ord_recv.at[slot])
        landed(maskv.at[slot - 1], mask_recv.at[slot - 1])
    token = lax.broadcasted_iota(jnp.int32, (slab, HD), 0)
    lane = lax.broadcasted_iota(jnp.int32, (slab, HD), 1)
    tile_tok = slab // tiles
    member = jnp.where(lax.div(token, tile_tok) == lane, 1.0, 0.0).astype(jnp.bfloat16)

    @pl.loop(0, 4)
    def _(slot):
        places = ordv[slot]

        @pl.loop(0, slab // HD)
        def _(block):
            row = lax.broadcasted_iota(jnp.int32, (HD, slab), 0) + block * HD
            match = jnp.where(places == row, 1.0, 0.0).astype(jnp.bfloat16)
            hot[slot, pl.ds(pl.multiple_of(block * HD, HD), HD), :] = jnp.dot(
                match, member, preferred_element_type=jnp.float32
            ).astype(jnp.bfloat16)

    tile_row = lax.broadcasted_iota(jnp.int32, (tiles, HD), 0)
    tile_lane = lax.broadcasted_iota(jnp.int32, (tiles, HD), 1)
    row_diff = lax.div(tile_lane, GW) - lax.div(tile_row, GW)
    col_diff = lax.rem(tile_lane, GW) - lax.rem(tile_row, GW)
    near_tiles = (jnp.abs(row_diff) <= 1) & (jnp.abs(col_diff) <= 1) & (tile_lane < tiles)
    place = (row_diff + 1) * 3 + col_diff + 1

    def mask_rows(slot):
        return jnp.concatenate([maskv[slot, tile] for tile in range(tiles)], axis=0)

    def bias_of(mask, shift):
        picked = jnp.zeros((tiles, HD), jnp.int32)
        for index in range(9):
            slot = shift * 9 + index
            picked = jnp.where(place == index, mask[:, slot : slot + 1], picked)
        return jnp.where(near_tiles & (picked == 1), 0.0, HIDDEN)

    def bias_rows(slot, bias):
        bias = jnp.concatenate([bias, jnp.zeros((HD - tiles, HD), jnp.float32)], axis=0)
        return jnp.dot(
            hot[slot], bias.astype(jnp.bfloat16), preferred_element_type=jnp.float32
        ).astype(jnp.bfloat16)

    for side in range(2):
        mask = mask_rows(side)
        for shift in range(3):
            qb[side, shift] = bias_rows(1 + side, bias_of(mask, shift))

    @pl.when(helps)
    def _():
        landed(maskv.at[2], mask_recv.at[2])
        mask = mask_rows(2)
        bias = jnp.where(helps_top, bias_of(mask, 0), bias_of(mask, 2))
        qbx[...] = bias_rows(jnp.where(helps_top, 3, 0), bias)

    def neighbour_copies(head):
        up = remote(kv.at[2, head], kv.at[0, head], zsend.at[0, head], kv_sem.at[0, head], to_up)
        down = remote(kv.at[1, head], kv.at[3, head], zsend.at[1, head], kv_sem.at[3, head], to_down)
        return up, down

    def query_copies(head):
        def one(device):
            return remote(qs.at[merged, head], qx.at[head], qx_send.at[head], qx_recv.at[head], device)

        return one(to_up), one(to_down)

    def partial_copies(head):
        def one(device):
            return (
                remote(sx.at[head], ox.at[head], ox_send.at[head], ox_recv.at[head], device),
                remote(sl.at[head], lx.at[head], lx_send.at[head], lx_recv.at[head], device),
            )

        return one(to_up), one(to_down)

    def pass_on(head):
        landed(kv.at[1, head], kv_sem.at[1, head])
        landed(kv.at[2, head], kv_sem.at[2, head])
        up, down = neighbour_copies(head)

        @pl.when(has_up & jnp.logical_not(helps_top))
        def _():
            up.start()

        @pl.when(has_down & jnp.logical_not(helps_bottom))
        def _():
            down.start()

        landed(qs.at[0, head], q_sem.at[0, head])
        landed(qs.at[1, head], q_sem.at[1, head])
        up, down = query_copies(head)

        @pl.when(bottom)
        def _():
            up.start()

        @pl.when(top)
        def _():
            down.start()

    def weight_copies(tile, step):
        ref = wt.at[tile, wt_rows(x, step)]
        return (
            remote(ref, ref, w_up.at[tile], w_recv.at[tile, step], to_up),
            remote(ref, ref, w_down.at[tile], w_recv.at[tile, step], to_down),
            remote(ref, ref, w_x.at[tile], x_recv.at[tile], to_x),
        )

    def relay(event):
        kind, step = lax.div(event, CHUNKS), lax.rem(event, CHUNKS)
        last = kind == 2 * planes - 2
        other = jnp.where(last, 1, lax.rem(kind, 2))
        distance = jnp.where(last, planes - 1, lax.div(kind, 2) + 1 - other)

        @pl.loop(0, 2)
        def _(way):
            plane = z + (2 * way - 1) * distance
            valid = (plane >= 0) & (plane < planes) & ((distance > 0) | (way == 0))

            @pl.when(valid)
            def _():
                tile = 2 * plane + y + other * (1 - 2 * y)
                landed(wt.at[tile, wt_rows(x, step)], w_recv.at[tile, step])
                up, down, across = weight_copies(tile, step)

                @pl.when((plane <= z) & has_up)
                def _():
                    up.start()

                @pl.when((plane >= z) & has_down)
                def _():
                    down.start()

                across.start()

    dims = (((1,), (1,)), ((), ()))
    ones = jnp.ones((slab, HD), jnp.bfloat16)

    def attend_rows(queries, biases, blocks, head):
        peak = total = None
        for bias, block in zip(biases, blocks):
            score = lax.dot_general(
                jnp.concatenate([queries, bias], axis=1),
                jnp.concatenate([kv[block, head, 0], hot[block]], axis=1),
                dims,
                preferred_element_type=jnp.float32,
            )
            before, peak = peak, jnp.max(score, axis=1, keepdims=True)
            if before is not None:
                peak = jnp.maximum(before, peak)
            part_sum = jnp.dot(
                jnp.exp2((score - peak) * factor).astype(jnp.bfloat16),
                jnp.concatenate([kv[block, head, 1], ones], axis=1),
                preferred_element_type=jnp.float32,
            )
            total = part_sum if before is None else total * jnp.exp2((before - peak) * factor) + part_sum
        denom = total[:, HD:]
        return total[:, :HD] / denom, peak * factor + jnp.log2(denom)

    def over_rows(action):
        @pl.loop(0, slab // ROWS)
        def _(block):
            action(pl.ds(pl.multiple_of(block * ROWS, ROWS), ROWS))

    def store(head, side, rows, value):
        value = value.astype(jnp.bfloat16)

        @pl.when(side == y)
        def _():
            att[rows, pl.ds(pl.multiple_of((y * half_heads + head) * HD, HD), HD)] = value

        @pl.when(side != y)
        def _():
            snd[head, rows, :] = value

    def attend_inner(head, side):
        def action(rows):
            biases = [qb[side, shift, rows, :] for shift in range(3)]
            blocks = [side + shift for shift in range(3)]
            value, _ = attend_rows(qs[side, head, rows, :], biases, blocks, head)
            store(head, side, rows, value)

        over_rows(action)

    def attend_end(head, side, merge):
        def action(rows):
            biases = [qb[side, index + 1 - side, rows, :] for index in range(2)]
            value, level = attend_rows(qs[side, head, rows, :], biases, (1, 2), head)
            if merge:
                other = jnp.broadcast_to(lx[head, 0:1, rows], (HD, ROWS)).T
                high = jnp.maximum(level, other)
                mine, theirs = jnp.exp2(level - high), jnp.exp2(other - high)
                value = (value * mine + ox[head, rows, :].astype(jnp.float32) * theirs) / (mine + theirs)
            store(head, side, rows, value)

        over_rows(action)

    def attend_for_end(head):
        block = jnp.where(helps_top, 2, 1)

        def action(rows):
            value, level = attend_rows(qx[head, rows, :], [qbx[rows, :]], (block,), head)
            sx[head, rows, :] = value.astype(jnp.bfloat16)
            sl[head, :, rows] = level.T[:8, :]

        over_rows(action)

    def result_copy(head):
        column = pl.ds(pl.multiple_of((y * half_heads + head) * HD, HD), HD)
        return remote(snd.at[head], att.at[:, column], a_send.at[head], a_recv.at[head], to_pair)

    def relays_before(point):
        return sum(jnp.where(point > index, many, 0) for index, many in enumerate(RELAYS))

    def relays_at(point):
        @pl.loop(relays_before(point), relays_before(point + 1))
        def _(event):
            relay(event)

    pass_on(0)
    relays_at(0)

    @pl.loop(0, half_heads)
    def _(head):
        @pl.when(head + 1 < half_heads)
        def _():
            pass_on(head + 1)

        @pl.when(helps)
        def _():
            landed(qx.at[head], qx_recv.at[head])
            attend_for_end(head)
            up, down = partial_copies(head)

            @pl.when(helps_top)
            def _():
                for copy in up:
                    copy.start()

            @pl.when(helps_bottom)
            def _():
                for copy in down:
                    copy.start()

        @pl.when(jnp.logical_not(is_end))
        def _():
            landed(kv.at[0, head], kv_sem.at[0, head])
            landed(kv.at[3, head], kv_sem.at[3, head])

        @pl.loop(0, 2)
        def _(turn):
            side = jnp.where(is_end, jnp.where(turn == 0, 1 - merged, merged), jnp.where(turn == 0, 1 - y, y))

            @pl.when(jnp.logical_not(is_end))
            def _():
                attend_inner(head, side)

            @pl.when(is_end & (turn == 0))
            def _():
                attend_end(head, side, False)

            @pl.when(is_end & (turn == 1))
            def _():
                landed(ox.at[head], ox_recv.at[head])
                landed(lx.at[head], lx_recv.at[head])
                attend_end(head, side, True)

            @pl.when(side != y)
            def _():
                result_copy(head).start()

            relays_at(1 + 2 * head + turn)

    done = sum(RELAYS)

    near.wait_send()
    mask_copy.wait_send()

    @pl.when(gives_mask)
    def _():
        mask_diag.wait_send()
        mask_far.wait_send()

    @pl.when(has_diag)
    def _():
        diag.wait_send()
        far.wait_send()

    @pl.loop(0, half_heads)
    def _(head):
        for copy in pair_copies(head):
            copy.wait_send()
        up, down = neighbour_copies(head)

        @pl.when(has_up & jnp.logical_not(helps_top))
        def _():
            up.wait_send()

        @pl.when(has_down & jnp.logical_not(helps_bottom))
        def _():
            down.wait_send()

        @pl.when(is_end)
        def _():
            query_copies(head)[0].wait_send()

        @pl.when(helps)
        def _():
            for copy in partial_copies(head)[0]:
                copy.wait_send()

    def left(ref, sem):
        remote(ref, ref, sem, x_recv.at[me], to_x).wait_send()

    left(wt_part(me, x), w_y)

    def sent_results():
        @pl.loop(0, half_heads)
        def _(head):
            result_copy(head).wait_send()

    def sent_weights():
        @pl.loop(0, count)
        def _(tile):
            plane = lax.div(tile, 2)

            @pl.when((plane <= z) & has_up)
            def _():
                left(wt_part(tile, x), w_up.at[tile])

            @pl.when((plane >= z) & has_down)
            def _():
                left(wt_part(tile, x), w_down.at[tile])

            @pl.when(tile != me)
            def _():
                left(wt_part(tile, x), w_x.at[tile])


    late = half_heads - LATE

    def results_landed(first, end):
        @pl.loop(first, end)
        def _(head):
            column = pl.ds(pl.multiple_of(((1 - y) * half_heads + head) * HD, HD), HD)
            landed(att.at[:, column], a_recv.at[head])

    results_landed(0, late)
    landed(wt.at[me], w_own)

    def partial_copy(tile):
        return remote(pb.at[tile], pr.at[tile], p_send.at[tile], p_recv.at[tile], to_core)

    def out_copy(plane):
        column = pl.ds(pl.multiple_of(plane * 2 * cols, 2 * cols), 2 * cols)
        return pltpu.make_async_copy(ob.at[plane], out_ref.at[:, column], o_sem.at[plane])

    def span(start, many):
        return pl.ds(pl.multiple_of(start * HD, HD), many * HD)

    def product(rows, plane, depth):
        left_side = att[rows, depth]
        sides = [wt[2 * plane + which, depth, :] for which in range(2)]
        if not aligned:
            return [jnp.dot(left_side, side, preferred_element_type=jnp.float32) for side in sides]
        both = jnp.dot(
            left_side, jnp.concatenate(sides, axis=1), preferred_element_type=jnp.float32
        )
        return both[:, :cols], both[:, cols:]

    own_span = span(y * half_heads, half_heads)
    early_span = span((1 - y) * half_heads, late)
    late_span = span((1 - y) * half_heads + late, LATE)
    given = pl.ds(pl.multiple_of((1 - core) * half, half), half)
    kept = pl.ds(pl.multiple_of(core * half, half), half)

    def project_early(plane):
        @pl.loop(0, 2)
        def _(which):
            tile = 2 * plane + which

            @pl.when(tile != me)
            def _():
                landed(wt_part(tile, 1 - x), x_recv.at[tile])

        rows = pl.ds(0, slab)
        sums = zip(product(rows, plane, own_span), product(rows, plane, early_span))
        for which, (first, second) in enumerate(sums):
            pe[2 * plane + which] = first + second

    def project_late(plane):
        for which, last in enumerate(product(given, plane, late_span)):
            tile = 2 * plane + which
            pb[tile] = (pe[tile, given, :] + last).astype(jnp.bfloat16)
            partial_copy(tile).start()

    def finish(plane):
        for which, last in enumerate(product(kept, plane, late_span)):
            tile = 2 * plane + which
            landed(pr.at[tile], p_recv.at[tile])
            total = pe[tile, kept, :] + last + pr[tile].astype(jnp.float32)
            total = total.astype(jnp.bfloat16)
            if aligned:
                out_ref[:, pl.ds(pl.multiple_of(tile * cols, HD), cols)] = total
            else:
                ob[plane, :, which * cols : (which + 1) * cols] = total
        if not aligned:
            out_copy(plane).start()

    def at_distance(distance, action):
        @pl.loop(0, 2)
        def _(way):
            plane = z + (2 * way - 1) * distance
            valid = (plane >= 0) & (plane < planes) & ((distance > 0) | (way == 0))

            @pl.when(valid)
            def _():
                action(plane)

    events = (2 * planes - 1) * CHUNKS

    def relay_for(distance):
        @pl.loop(0, 2 * CHUNKS)
        def _(index):
            event = (2 * distance + 2) * CHUNKS + index

            @pl.when((event >= done) & (event < events))
            def _():
                relay(event)

    @pl.loop(0, EARLY_DISTANCE + 1)
    def _(distance):
        relay_for(distance)
        at_distance(distance, project_early)

    results_landed(late, half_heads)

    @pl.loop(0, EARLY_DISTANCE + 1)
    def _(distance):
        at_distance(distance, project_late)

    @pl.loop(0, EARLY_DISTANCE)
    def _(distance):
        at_distance(distance, finish)

    @pl.loop(EARLY_DISTANCE + 1, planes)
    def _(distance):
        relay_for(distance)
        at_distance(distance, project_early)
        at_distance(distance, project_late)
        at_distance(distance - 1, finish)

    at_distance(planes - 1, finish)

    sent_results()
    sent_weights()

    @pl.loop(0, count)
    def _(tile):
        partial_copy(tile).wait_send()

    if not aligned:
        @pl.loop(0, planes)
        def _(plane):
            out_copy(plane).wait()


def on_device(query, key, value, tile_mask, order, out_weight):
    slab, width = query.shape
    tiles = tile_mask.shape[1]
    heads = width // HD
    count = lax.axis_size("tm")
    cols = out_weight.shape[1]
    half_heads = heads // 2
    planes = count // 2
    half = slab // 2
    bf16, f32 = jnp.bfloat16, jnp.float32
    dma = pltpu.SemaphoreType.DMA
    scratch = [
        pltpu.VMEM((4, half_heads, 2, slab, HD), bf16),
        pltpu.VMEM((2, half_heads, slab, HD), bf16),
        pltpu.VMEM((4, slab, HD), bf16),
        pltpu.VMEM((2, 3, slab, HD), bf16),
        pltpu.VMEM((4, 1, slab), jnp.int32),
        pltpu.VMEM((3, tiles, 1, tile_mask.shape[2]), jnp.int32),
        pltpu.VMEM((count, width, cols), bf16),
        pltpu.VMEM((slab, width), bf16),
        pltpu.VMEM((half_heads, slab, HD), bf16),
        pltpu.VMEM((half_heads, slab, HD), bf16),
        pltpu.VMEM((slab, HD), bf16),
        pltpu.VMEM((half_heads, slab, HD), bf16),
        pltpu.VMEM((half_heads, 8, slab), f32),
        pltpu.VMEM((half_heads, slab, HD), bf16),
        pltpu.VMEM((half_heads, 8, slab), f32),
        pltpu.VMEM((count, slab, cols), f32),
        pltpu.VMEM((count, half, cols), bf16),
        pltpu.VMEM((count, half, cols), bf16),
        pltpu.VMEM((planes, half, 2 * cols) if cols % HD else (8, HD), bf16),
        dma((4, half_heads)),
        dma((2, half_heads)),
        dma((half_heads, 3)),
        dma((2, half_heads)),
        dma((4,)),
        dma((3,)),
        dma((3,)),
        dma((3,)),
        dma((count, CHUNKS)),
        dma((count,)),
        dma((count,)),
        dma((count,)),
        dma((count,)),
        dma,
        dma,
        dma((half_heads,)),
        dma((half_heads,)),
        dma((count,)),
        dma((count,)),
        dma((planes,)),
        dma((half_heads,)),
        dma((half_heads,)),
        dma((half_heads,)),
        dma((half_heads,)),
        dma((half_heads,)),
        dma((half_heads,)),
    ]
    sizes = (count, heads, slab, tiles, width, cols)
    return pl.pallas_call(
        functools.partial(kernel, sizes),
        in_specs=[pl.BlockSpec(memory_space=pltpu.HBM)] * 6,
        out_specs=pl.BlockSpec(memory_space=pltpu.VMEM),
        out_shape=pltpu.VMEM((half, count * cols), bf16),
        scratch_shapes=scratch,
        compiler_params=pltpu.CompilerParams(
            collective_id=0, has_side_effects=True, vmem_limit_bytes=58 << 20
        ),
        cost_estimate=pl.CostEstimate(
            flops=4 * heads * slab * 3 * slab * HD + 2 * slab * width * count * cols,
            bytes_accessed=8 * slab * width,
            transcendentals=heads * slab * 3 * slab,
        ),
        name="clip_attention",
    )(query, key, value, tile_mask.transpose(1, 0, 2), order, out_weight)


def solution(mesh):
    placed = (
        P(("clips", "tm"), "head"),
        P(("clips", "tm"), "head"),
        P(("clips", "tm"), "head"),
        P(("clips", "tm"), None, None),
        P(("clips", "tm"), None),
        P(None, "tm"),
    )
    return jax.shard_map(
        on_device,
        mesh=mesh,
        in_specs=placed,
        out_specs=P(("clips", "tm", "head"), None),
        check_vma=False,
    )
```

```python
import functools
import math

import jax
import jax.numpy as jnp
from jax import lax
from jax.experimental import pallas as pl
from jax.experimental.pallas import tpu as pltpu
from jax.sharding import PartitionSpec as P

HD = 128
GW = 3
HIDDEN = -1e30
CHUNKS = 3
ROWS = 768
LATE = 2
EARLY_DISTANCE = 3
OWN_WEIGHT_AFTER = (0, 0, 1)
RELAYS = (5, 3, 0, 0, 2, 5, 0, 2, 0, 4, 0, 0, 0)
MESH = pl.DeviceIdType.MESH


def kernel(sizes, q_hbm, k_hbm, v_hbm, mask_hbm, order_hbm, w_hbm, out_ref, *scratch):
    count, heads, slab, tiles, width, cols = sizes
    (kv, qs, hot, qb, ordv, maskv, wt, att, snd, qx, qbx, ox, lx, sx, sl, pe, pb, pr, ob,
     kv_sem, q_sem, ysend, zsend, ord_recv, ord_send, mask_recv, mask_send,
     w_recv, x_recv, w_up, w_down, w_x, w_y, w_own,
     a_recv, a_send, p_recv, p_send, o_sem,
     qx_recv, qx_send, ox_recv, ox_send, lx_recv, lx_send) = scratch
    half_heads = heads // 2
    planes = count // 2
    part = width // 2
    piece = part // CHUNKS
    half = slab // 2
    aligned = cols % HD == 0
    factor = HD ** (-0.5) * math.log2(math.e)

    clip = lax.axis_index("clips")
    me = lax.axis_index("tm")
    core = lax.axis_index("head")
    x = lax.rem(clip, 2)
    z = lax.div(me, 2)
    y = lax.rem(me, 2)
    pair = me + 1 - 2 * y
    sign = 2 * y - 1
    has_up = z < planes - 1
    has_down = z > 0
    has_diag = (z + sign >= 0) & (z + sign < planes)
    top, bottom = z == planes - 1, z == 0
    is_end = top | bottom
    helps_top, helps_bottom = z == planes - 2, z == 1
    helps = helps_top | helps_bottom
    merged = jnp.where(top, 0, 1)

    to_pair = (clip, pair, core)
    to_up = (clip, me + 2, core)
    to_down = (clip, me - 2, core)
    to_diag = (clip, me + sign, core)
    to_far = (clip, me + 2 * sign, core)
    to_x = (clip + 1 - 2 * x, me, core)
    to_core = (clip, me, 1 - core)

    def remote(src, dst, send, recv, device):
        return pltpu.make_async_remote_copy(
            src_ref=src, dst_ref=dst, send_sem=send, recv_sem=recv,
            device_id=device, device_id_type=MESH,
        )

    def landed(ref, sem):
        pltpu.make_async_copy(ref, ref, sem).wait()

    barrier = pltpu.get_barrier_semaphore()
    for device in (to_pair, to_x, to_core):
        pl.semaphore_signal(barrier, inc=1, device_id=device, device_id_type=MESH)
    for device, valid in ((to_up, has_up), (to_down, has_down), (to_diag, has_diag)):
        @pl.when(valid)
        def _():
            pl.semaphore_signal(barrier, inc=1, device_id=device, device_id_type=MESH)
    pl.semaphore_wait(
        barrier,
        3 + has_up.astype(jnp.int32) + has_down.astype(jnp.int32) + has_diag.astype(jnp.int32),
    )

    def order_copies():
        near = remote(order_hbm, ordv.at[1 + y], ord_send.at[0], ord_recv.at[1 + y], to_pair)
        slot = 3 - 3 * y
        diag = remote(order_hbm, ordv.at[slot], ord_send.at[1], ord_recv.at[slot], to_diag)
        far = remote(order_hbm, ordv.at[slot], ord_send.at[2], ord_recv.at[slot], to_far)
        return near, diag, far

    mask_copy = remote(mask_hbm, maskv.at[y], mask_send.at[0], mask_recv.at[y], to_pair)
    mask_diag = remote(mask_hbm, maskv.at[2], mask_send.at[1], mask_recv.at[2], to_diag)
    mask_far = remote(mask_hbm, maskv.at[2], mask_send.at[2], mask_recv.at[2], to_far)
    gives_mask = is_end & has_diag
    near, diag, far = order_copies()
    near.start()
    mask_copy.start()

    @pl.when(has_diag)
    def _():
        diag.start()
        far.start()

    @pl.when(gives_mask)
    def _():
        mask_diag.start()
        mask_far.start()

    def pair_copies(head):
        column = pl.ds(pl.multiple_of(((1 - y) * half_heads + head) * HD, HD), HD)
        return [
            remote(k_hbm.at[:, column], kv.at[1 + y, head, 0], ysend.at[head, 0],
                   kv_sem.at[1 + y, head], to_pair),
            remote(v_hbm.at[:, column], kv.at[1 + y, head, 1], ysend.at[head, 1],
                   kv_sem.at[1 + y, head], to_pair),
            remote(q_hbm.at[:, column], qs.at[y, head], ysend.at[head, 2],
                   q_sem.at[y, head], to_pair),
        ]

    def own_rows(step):
        return pl.ds(pl.multiple_of(core * width + x * part + step * piece, piece), piece)

    def wt_rows(side, step):
        return pl.ds(pl.multiple_of(side * part + step * piece, piece), piece)

    def wt_part(tile, side):
        return wt.at[tile, pl.ds(pl.multiple_of(side * part, part), part)]

    def own_weight_copies(step):
        src = w_hbm.at[own_rows(step)]
        dst = wt.at[me, wt_rows(x, step)]
        recv = w_recv.at[me, step]
        return (
            remote(src, dst, w_y, recv, to_pair),
            remote(src, dst, w_up.at[me], recv, to_up),
            remote(src, dst, w_down.at[me], recv, to_down),
        )

    own_weight = pltpu.make_async_copy(
        w_hbm.at[pl.ds(pl.multiple_of(core * width, width), width)], wt.at[me], w_own)

    @pl.loop(0, half_heads)
    def _(head):
        for copy in pair_copies(head):
            copy.start()

        for step in range(CHUNKS):
            @pl.when(head == OWN_WEIGHT_AFTER[step])
            def _():
                own_weight_copies(step)[0].start()

    @pl.loop(0, CHUNKS)
    def _(step):
        _, up, down = own_weight_copies(step)

        @pl.when(has_up)
        def _():
            up.start()

        @pl.when(has_down)
        def _():
            down.start()

    pltpu.make_async_copy(order_hbm, ordv.at[1 + y], ord_recv.at[1 + y]).start()
    pltpu.make_async_copy(mask_hbm, maskv.at[y], mask_recv.at[y]).start()

    @pl.loop(0, half_heads)
    def _(head):
        column = pl.ds(pl.multiple_of((y * half_heads + head) * HD, HD), HD)
        pltpu.make_async_copy(k_hbm.at[:, column], kv.at[1 + y, head, 0], kv_sem.at[1 + y, head]).start()
        pltpu.make_async_copy(v_hbm.at[:, column], kv.at[1 + y, head, 1], kv_sem.at[1 + y, head]).start()
        pltpu.make_async_copy(q_hbm.at[:, column], qs.at[y, head], q_sem.at[y, head]).start()

    own_weight.start()

    @pl.when(bottom)
    def _():
        ordv[0] = lax.broadcasted_iota(jnp.int32, (1, slab), 1)

    @pl.when(top)
    def _():
        ordv[3] = lax.broadcasted_iota(jnp.int32, (1, slab), 1)

    @pl.when(has_down)
    def _():
        landed(ordv.at[0], ord_recv.at[0])

    @pl.when(has_up)
    def _():
        landed(ordv.at[3], ord_recv.at[3])

    for slot in (1, 2):
        landed(ordv.at[slot], ord_recv.at[slot])
        landed(maskv.at[slot - 1], mask_recv.at[slot - 1])
    token = lax.broadcasted_iota(jnp.int32, (slab, HD), 0)
    lane = lax.broadcasted_iota(jnp.int32, (slab, HD), 1)
    tile_tok = slab // tiles
    member = jnp.where(lax.div(token, tile_tok) == lane, 1.0, 0.0).astype(jnp.bfloat16)

    @pl.loop(0, 4)
    def _(slot):
        places = ordv[slot]

        @pl.loop(0, slab // HD)
        def _(block):
            row = lax.broadcasted_iota(jnp.int32, (HD, slab), 0) + block * HD
            match = jnp.where(places == row, 1.0, 0.0).astype(jnp.bfloat16)
            hot[slot, pl.ds(pl.multiple_of(block * HD, HD), HD), :] = jnp.dot(
                match, member, preferred_element_type=jnp.float32
            ).astype(jnp.bfloat16)

    tile_row = lax.broadcasted_iota(jnp.int32, (tiles, HD), 0)
    tile_lane = lax.broadcasted_iota(jnp.int32, (tiles, HD), 1)
    row_diff = lax.div(tile_lane, GW) - lax.div(tile_row, GW)
    col_diff = lax.rem(tile_lane, GW) - lax.rem(tile_row, GW)
    near_tiles = (jnp.abs(row_diff) <= 1) & (jnp.abs(col_diff) <= 1) & (tile_lane < tiles)
    place = (row_diff + 1) * 3 + col_diff + 1

    def mask_rows(slot):
        return jnp.concatenate([maskv[slot, tile] for tile in range(tiles)], axis=0)

    def bias_of(mask, shift):
        picked = jnp.zeros((tiles, HD), jnp.int32)
        for index in range(9):
            slot = shift * 9 + index
            picked = jnp.where(place == index, mask[:, slot : slot + 1], picked)
        return jnp.where(near_tiles & (picked == 1), 0.0, HIDDEN)

    def bias_rows(slot, bias):
        bias = jnp.concatenate([bias, jnp.zeros((HD - tiles, HD), jnp.float32)], axis=0)
        return jnp.dot(
            hot[slot], bias.astype(jnp.bfloat16), preferred_element_type=jnp.float32
        ).astype(jnp.bfloat16)

    for side in range(2):
        mask = mask_rows(side)
        for shift in range(3):
            qb[side, shift] = bias_rows(1 + side, bias_of(mask, shift))

    @pl.when(helps)
    def _():
        landed(maskv.at[2], mask_recv.at[2])
        mask = mask_rows(2)
        bias = jnp.where(helps_top, bias_of(mask, 0), bias_of(mask, 2))
        qbx[...] = bias_rows(jnp.where(helps_top, 3, 0), bias)

    def neighbour_copies(head):
        up = remote(kv.at[2, head], kv.at[0, head], zsend.at[0, head], kv_sem.at[0, head], to_up)
        down = remote(kv.at[1, head], kv.at[3, head], zsend.at[1, head], kv_sem.at[3, head], to_down)
        return up, down

    def query_copies(head):
        def one(device):
            return remote(qs.at[merged, head], qx.at[head], qx_send.at[head], qx_recv.at[head], device)

        return one(to_up), one(to_down)

    def partial_copies(head):
        def one(device):
            return (
                remote(sx.at[head], ox.at[head], ox_send.at[head], ox_recv.at[head], device),
                remote(sl.at[head], lx.at[head], lx_send.at[head], lx_recv.at[head], device),
            )

        return one(to_up), one(to_down)

    def pass_on(head):
        landed(kv.at[1, head], kv_sem.at[1, head])
        landed(kv.at[2, head], kv_sem.at[2, head])
        up, down = neighbour_copies(head)

        @pl.when(has_up & jnp.logical_not(helps_top))
        def _():
            up.start()

        @pl.when(has_down & jnp.logical_not(helps_bottom))
        def _():
            down.start()

        landed(qs.at[0, head], q_sem.at[0, head])
        landed(qs.at[1, head], q_sem.at[1, head])
        up, down = query_copies(head)

        @pl.when(bottom)
        def _():
            up.start()

        @pl.when(top)
        def _():
            down.start()

    def weight_copies(tile, step):
        ref = wt.at[tile, wt_rows(x, step)]
        return (
            remote(ref, ref, w_up.at[tile], w_recv.at[tile, step], to_up),
            remote(ref, ref, w_down.at[tile], w_recv.at[tile, step], to_down),
            remote(ref, ref, w_x.at[tile], x_recv.at[tile], to_x),
        )

    def relay(event):
        kind, step = lax.div(event, CHUNKS), lax.rem(event, CHUNKS)
        last = kind == 2 * planes - 2
        other = jnp.where(last, 1, lax.rem(kind, 2))
        distance = jnp.where(last, planes - 1, lax.div(kind, 2) + 1 - other)

        @pl.loop(0, 2)
        def _(way):
            plane = z + (2 * way - 1) * distance
            valid = (plane >= 0) & (plane < planes) & ((distance > 0) | (way == 0))

            @pl.when(valid)
            def _():
                tile = 2 * plane + y + other * (1 - 2 * y)
                landed(wt.at[tile, wt_rows(x, step)], w_recv.at[tile, step])
                up, down, across = weight_copies(tile, step)

                @pl.when((plane <= z) & has_up)
                def _():
                    up.start()

                @pl.when((plane >= z) & has_down)
                def _():
                    down.start()

                across.start()

    dims = (((1,), (1,)), ((), ()))
    ones = jnp.ones((slab, HD), jnp.bfloat16)

    def attend_rows(queries, biases, blocks, head):
        peak = total = None
        for bias, block in zip(biases, blocks):
            score = lax.dot_general(
                jnp.concatenate([queries, bias], axis=1),
                jnp.concatenate([kv[block, head, 0], hot[block]], axis=1),
                dims,
                preferred_element_type=jnp.float32,
            )
            before, peak = peak, jnp.max(score, axis=1, keepdims=True)
            if before is not None:
                peak = jnp.maximum(before, peak)
            part_sum = jnp.dot(
                jnp.exp2((score - peak) * factor).astype(jnp.bfloat16),
                jnp.concatenate([kv[block, head, 1], ones], axis=1),
                preferred_element_type=jnp.float32,
            )
            total = part_sum if before is None else total * jnp.exp2((before - peak) * factor) + part_sum
        denom = total[:, HD:]
        return total[:, :HD] / denom, peak * factor + jnp.log2(denom)

    def over_rows(action):
        @pl.loop(0, slab // ROWS)
        def _(block):
            action(pl.ds(pl.multiple_of(block * ROWS, ROWS), ROWS))

    def store(head, side, rows, value):
        value = value.astype(jnp.bfloat16)

        @pl.when(side == y)
        def _():
            att[rows, pl.ds(pl.multiple_of((y * half_heads + head) * HD, HD), HD)] = value

        @pl.when(side != y)
        def _():
            snd[head, rows, :] = value

    def attend_inner(head, side):
        def action(rows):
            biases = [qb[side, shift, rows, :] for shift in range(3)]
            blocks = [side + shift for shift in range(3)]
            value, _ = attend_rows(qs[side, head, rows, :], biases, blocks, head)
            store(head, side, rows, value)

        over_rows(action)

    def attend_end(head, side, merge):
        def action(rows):
            biases = [qb[side, index + 1 - side, rows, :] for index in range(2)]
            value, level = attend_rows(qs[side, head, rows, :], biases, (1, 2), head)
            if merge:
                other = jnp.broadcast_to(lx[head, 0:1, rows], (HD, ROWS)).T
                high = jnp.maximum(level, other)
                mine, theirs = jnp.exp2(level - high), jnp.exp2(other - high)
                value = (value * mine + ox[head, rows, :].astype(jnp.float32) * theirs) / (mine + theirs)
            store(head, side, rows, value)

        over_rows(action)

    def attend_for_end(head):
        block = jnp.where(helps_top, 2, 1)

        def action(rows):
            value, level = attend_rows(qx[head, rows, :], [qbx[rows, :]], (block,), head)
            sx[head, rows, :] = value.astype(jnp.bfloat16)
            sl[head, :, rows] = level.T[:8, :]

        over_rows(action)

    def result_copy(head):
        column = pl.ds(pl.multiple_of((y * half_heads + head) * HD, HD), HD)
        return remote(snd.at[head], att.at[:, column], a_send.at[head], a_recv.at[head], to_pair)

    def relays_before(point):
        return sum(jnp.where(point > index, many, 0) for index, many in enumerate(RELAYS))

    def relays_at(point):
        @pl.loop(relays_before(point), relays_before(point + 1))
        def _(event):
            relay(event)

    pass_on(0)
    relays_at(0)

    @pl.loop(0, half_heads)
    def _(head):
        @pl.when(head + 1 < half_heads)
        def _():
            pass_on(head + 1)

        @pl.when(helps)
        def _():
            landed(qx.at[head], qx_recv.at[head])
            attend_for_end(head)
            up, down = partial_copies(head)

            @pl.when(helps_top)
            def _():
                for copy in up:
                    copy.start()

            @pl.when(helps_bottom)
            def _():
                for copy in down:
                    copy.start()

        @pl.when(jnp.logical_not(is_end))
        def _():
            landed(kv.at[0, head], kv_sem.at[0, head])
            landed(kv.at[3, head], kv_sem.at[3, head])

        @pl.loop(0, 2)
        def _(turn):
            side = jnp.where(is_end, jnp.where(turn == 0, 1 - merged, merged), jnp.where(turn == 0, 1 - y, y))

            @pl.when(jnp.logical_not(is_end))
            def _():
                attend_inner(head, side)

            @pl.when(is_end & (turn == 0))
            def _():
                attend_end(head, side, False)

            @pl.when(is_end & (turn == 1))
            def _():
                landed(ox.at[head], ox_recv.at[head])
                landed(lx.at[head], lx_recv.at[head])
                attend_end(head, side, True)

            @pl.when(side != y)
            def _():
                result_copy(head).start()

            relays_at(1 + 2 * head + turn)

    done = sum(RELAYS)

    near.wait_send()
    mask_copy.wait_send()

    @pl.when(gives_mask)
    def _():
        mask_diag.wait_send()
        mask_far.wait_send()

    @pl.when(has_diag)
    def _():
        diag.wait_send()
        far.wait_send()

    @pl.loop(0, half_heads)
    def _(head):
        for copy in pair_copies(head):
            copy.wait_send()
        up, down = neighbour_copies(head)

        @pl.when(has_up & jnp.logical_not(helps_top))
        def _():
            up.wait_send()

        @pl.when(has_down & jnp.logical_not(helps_bottom))
        def _():
            down.wait_send()

        @pl.when(is_end)
        def _():
            query_copies(head)[0].wait_send()

        @pl.when(helps)
        def _():
            for copy in partial_copies(head)[0]:
                copy.wait_send()

    def left(ref, sem):
        remote(ref, ref, sem, x_recv.at[me], to_x).wait_send()

    left(wt_part(me, x), w_y)

    def sent_results():
        @pl.loop(0, half_heads)
        def _(head):
            result_copy(head).wait_send()

    def sent_weights():
        @pl.loop(0, count)
        def _(tile):
            plane = lax.div(tile, 2)

            @pl.when((plane <= z) & has_up)
            def _():
                left(wt_part(tile, x), w_up.at[tile])

            @pl.when((plane >= z) & has_down)
            def _():
                left(wt_part(tile, x), w_down.at[tile])

            @pl.when(tile != me)
            def _():
                left(wt_part(tile, x), w_x.at[tile])


    late = half_heads - LATE

    def results_landed(first, end):
        @pl.loop(first, end)
        def _(head):
            column = pl.ds(pl.multiple_of(((1 - y) * half_heads + head) * HD, HD), HD)
            landed(att.at[:, column], a_recv.at[head])

    results_landed(0, late)
    landed(wt.at[me], w_own)

    def partial_copy(tile):
        return remote(pb.at[tile], pr.at[tile], p_send.at[tile], p_recv.at[tile], to_core)

    def out_copy(plane):
        column = pl.ds(pl.multiple_of(plane * 2 * cols, 2 * cols), 2 * cols)
        return pltpu.make_async_copy(ob.at[plane], out_ref.at[:, column], o_sem.at[plane])

    def span(start, many):
        return pl.ds(pl.multiple_of(start * HD, HD), many * HD)

    def product(rows, plane, depth):
        left_side = att[rows, depth]
        sides = [wt[2 * plane + which, depth, :] for which in range(2)]
        if not aligned:
            return [jnp.dot(left_side, side, preferred_element_type=jnp.float32) for side in sides]
        both = jnp.dot(
            left_side, jnp.concatenate(sides, axis=1), preferred_element_type=jnp.float32
        )
        return both[:, :cols], both[:, cols:]

    own_span = span(y * half_heads, half_heads)
    early_span = span((1 - y) * half_heads, late)
    late_span = span((1 - y) * half_heads + late, LATE)
    given = pl.ds(pl.multiple_of((1 - core) * half, half), half)
    kept = pl.ds(pl.multiple_of(core * half, half), half)

    def project_early(plane):
        @pl.loop(0, 2)
        def _(which):
            tile = 2 * plane + which

            @pl.when(tile != me)
            def _():
                landed(wt_part(tile, 1 - x), x_recv.at[tile])

        rows = pl.ds(0, slab)
        sums = zip(product(rows, plane, own_span), product(rows, plane, early_span))
        for which, (first, second) in enumerate(sums):
            pe[2 * plane + which] = first + second

    def project_late(plane):
        for which, last in enumerate(product(given, plane, late_span)):
            tile = 2 * plane + which
            pb[tile] = (pe[tile, given, :] + last).astype(jnp.bfloat16)
            partial_copy(tile).start()

    def finish(plane):
        for which, last in enumerate(product(kept, plane, late_span)):
            tile = 2 * plane + which
            landed(pr.at[tile], p_recv.at[tile])
            total = pe[tile, kept, :] + last + pr[tile].astype(jnp.float32)
            total = total.astype(jnp.bfloat16)
            if aligned:
                out_ref[:, pl.ds(pl.multiple_of(tile * cols, HD), cols)] = total
            else:
                ob[plane, :, which * cols : (which + 1) * cols] = total
        if not aligned:
            out_copy(plane).start()

    def at_distance(distance, action):
        @pl.loop(0, 2)
        def _(way):
            plane = z + (2 * way - 1) * distance
            valid = (plane >= 0) & (plane < planes) & ((distance > 0) | (way == 0))

            @pl.when(valid)
            def _():
                action(plane)

    events = (2 * planes - 1) * CHUNKS

    def relay_for(distance):
        @pl.loop(0, 2 * CHUNKS)
        def _(index):
            event = (2 * distance + 2) * CHUNKS + index

            @pl.when((event >= done) & (event < events))
            def _():
                relay(event)

    @pl.loop(0, EARLY_DISTANCE + 1)
    def _(distance):
        relay_for(distance)
        at_distance(distance, project_early)

    results_landed(late, half_heads)

    @pl.loop(0, EARLY_DISTANCE + 1)
    def _(distance):
        at_distance(distance, project_late)

    all_relayed = planes <= EARLY_DISTANCE + 1
    if all_relayed:
        sent_results()
        sent_weights()

    @pl.loop(0, EARLY_DISTANCE)
    def _(distance):
        at_distance(distance, finish)

    @pl.loop(EARLY_DISTANCE + 1, planes)
    def _(distance):
        relay_for(distance)
        at_distance(distance, project_early)
        at_distance(distance, project_late)
        at_distance(distance - 1, finish)

    at_distance(planes - 1, finish)

    if not all_relayed:
        sent_results()
        sent_weights()

    @pl.loop(0, count)
    def _(tile):
        partial_copy(tile).wait_send()

    if not aligned:
        @pl.loop(0, planes)
        def _(plane):
            out_copy(plane).wait()


def on_device(query, key, value, tile_mask, order, out_weight):
    slab, width = query.shape
    tiles = tile_mask.shape[1]
    heads = width // HD
    count = lax.axis_size("tm")
    cols = out_weight.shape[1]
    half_heads = heads // 2
    planes = count // 2
    half = slab // 2
    bf16, f32 = jnp.bfloat16, jnp.float32
    dma = pltpu.SemaphoreType.DMA
    scratch = [
        pltpu.VMEM((4, half_heads, 2, slab, HD), bf16),
        pltpu.VMEM((2, half_heads, slab, HD), bf16),
        pltpu.VMEM((4, slab, HD), bf16),
        pltpu.VMEM((2, 3, slab, HD), bf16),
        pltpu.VMEM((4, 1, slab), jnp.int32),
        pltpu.VMEM((3, tiles, 1, tile_mask.shape[2]), jnp.int32),
        pltpu.VMEM((count, width, cols), bf16),
        pltpu.VMEM((slab, width), bf16),
        pltpu.VMEM((half_heads, slab, HD), bf16),
        pltpu.VMEM((half_heads, slab, HD), bf16),
        pltpu.VMEM((slab, HD), bf16),
        pltpu.VMEM((half_heads, slab, HD), bf16),
        pltpu.VMEM((half_heads, 8, slab), f32),
        pltpu.VMEM((half_heads, slab, HD), bf16),
        pltpu.VMEM((half_heads, 8, slab), f32),
        pltpu.VMEM((count, slab, cols), f32),
        pltpu.VMEM((count, half, cols), bf16),
        pltpu.VMEM((count, half, cols), bf16),
        pltpu.VMEM((planes, half, 2 * cols) if cols % HD else (8, HD), bf16),
        dma((4, half_heads)),
        dma((2, half_heads)),
        dma((half_heads, 3)),
        dma((2, half_heads)),
        dma((4,)),
        dma((3,)),
        dma((3,)),
        dma((3,)),
        dma((count, CHUNKS)),
        dma((count,)),
        dma((count,)),
        dma((count,)),
        dma((count,)),
        dma,
        dma,
        dma((half_heads,)),
        dma((half_heads,)),
        dma((count,)),
        dma((count,)),
        dma((planes,)),
        dma((half_heads,)),
        dma((half_heads,)),
        dma((half_heads,)),
        dma((half_heads,)),
        dma((half_heads,)),
        dma((half_heads,)),
    ]
    sizes = (count, heads, slab, tiles, width, cols)
    return pl.pallas_call(
        functools.partial(kernel, sizes),
        in_specs=[pl.BlockSpec(memory_space=pltpu.HBM)] * 6,
        out_specs=pl.BlockSpec(memory_space=pltpu.VMEM),
        out_shape=pltpu.VMEM((half, count * cols), bf16),
        scratch_shapes=scratch,
        compiler_params=pltpu.CompilerParams(
            collective_id=0, has_side_effects=True, vmem_limit_bytes=58 << 20
        ),
        cost_estimate=pl.CostEstimate(
            flops=4 * heads * slab * 3 * slab * HD + 2 * slab * width * count * cols,
            bytes_accessed=8 * slab * width,
            transcendentals=heads * slab * 3 * slab,
        ),
        name="clip_attention",
    )(query, key, value, tile_mask.transpose(1, 0, 2), order, out_weight)


def solution(mesh):
    placed = (
        P(("clips", "tm"), "head"),
        P(("clips", "tm"), "head"),
        P(("clips", "tm"), "head"),
        P(("clips", "tm"), None, None),
        P(("clips", "tm"), None),
        P(None, "tm"),
    )
    return jax.shard_map(
        on_device,
        mesh=mesh,
        in_specs=placed,
        out_specs=P(("clips", "tm", "head"), None),
        check_vma=False,
    )
```
